512 devices in a mesh: vert: 64 (over x, y, core), frame: 8 (over z).
Axes of the slice: x: 4, y: 8, z: 8, core: 2. Of those that a mesh axis runs over, the one named last changes fastest.
Arguments:
- animated: float32 [1024, 3, 131072], P('frame', None, 'vert'), may hold values from -10 to 10
- rest_positions: float32 [3, 131072], P(None, 'vert'), may hold values from -4 to 4
- labels: int32 [131072], P('vert'), may hold values from 0 to 63
- weight_prior: float32 [64, 131072], P(None, 'vert'), may hold values from 0.002 to 0.12
Outputs:
- new_weights: float32 [64, 131072], P(None, 'vert')
- fit_error: float32 [], replicated
The draws below stay inside these ranges and needn't reach their ends.
All inputs are finite; a program needn't handle non-finite values.
Results may differ from the reference program's by a relative error of at most 0.0005.
Values sent between devices are 32-bit elements; how exact they have to be, the bound alone decides.
A program may use at most 64 MiB of HBM per device.

```python
import math
import jax
import jax.numpy as jnp
from jax import lax

B = 64
FR_DEV = 128
VERTS = 131072
FRAMES = 1024
N_FRAME = 8


def label_draw(key):
    base = jax.random.fold_in(key, 21)
    first = jax.random.randint(jax.random.fold_in(base, 1), (VERTS,), 0, B)
    second = jax.random.randint(jax.random.fold_in(base, 2), (VERTS,), 0, B)
    order = jax.random.permutation(jax.random.fold_in(base, 3), B)
    return jnp.take(order, jnp.minimum(first, second)).astype(jnp.int32)


def base_rest(key):
    labels = label_draw(key)
    centres = jax.random.uniform(jax.random.fold_in(key, 22), (3, B), jnp.float32, -2.5, 2.5)
    picked = jnp.take(centres, labels, axis=1)
    offsets = 0.5 * jnp.clip(jax.random.normal(jax.random.fold_in(key, 11), (3, VERTS), jnp.float32), -3.0, 3.0)
    return jnp.clip(picked + offsets, -4.0, 4.0)


def draw_labels(key, part):
    return label_draw(key)


def draw_rest_positions(key, part):
    return base_rest(key)


def draw_weight_prior(key, part):
    levels = jnp.exp(jax.random.uniform(jax.random.fold_in(key, 31), (B, 1), jnp.float32, math.log(0.004), math.log(0.06)))
    factor = jnp.exp(jax.random.uniform(jax.random.fold_in(key, 32), (B, VERTS), jnp.float32, -math.log(2.0), math.log(2.0)))
    return levels * factor


def draw_animated(key, part):
    rest = base_rest(key)
    scales = jax.random.uniform(jax.random.fold_in(key, 12), (FRAMES, 3, 1), jnp.float32, 0.5, 1.5)
    ramp = jnp.arange(FRAMES, dtype=jnp.float32).reshape(FRAMES, 1, 1) / (FRAMES - 1.0)
    jitter = jax.random.uniform(jax.random.fold_in(key, 14), (FRAMES, 1, 1), jnp.float32, 0.8, 1.2)
    level = 0.35 * jnp.exp(ramp * math.log(3.0)) * jitter
    noise = jnp.clip(jax.random.normal(jax.random.fold_in(key, 13), (FRAMES, 3, VERTS), jnp.float32), -3.0, 3.0)
    return rest[None, :, :] * scales + level * noise


def setup_inputs(seed: int = 0) -> dict:
    streams_of = jax.random.split(jax.random.key(seed), 5)
    return {
        "animated": draw_animated(jax.random.fold_in(streams_of[4], 71), 0),
        "rest_positions": draw_rest_positions(jax.random.fold_in(streams_of[4], 71), 0),
        "labels": draw_labels(jax.random.fold_in(streams_of[4], 71), 0),
        "weight_prior": draw_weight_prior(jax.random.fold_in(streams_of[4], 71), 0),
    }


ridge_scale = 0.0001
step_size = 0.005

def bone_features(weights, homogeneous):
    return (weights[:, None, :] * homogeneous[None, :, :]).reshape(4 * weights.shape[0], weights.shape[1])

def start_weights(labels, weight_prior):
    bones = weight_prior.shape[0]
    onehot = (labels[None, :] == jnp.arange(bones, dtype=jnp.int32)[:, None]).astype(jnp.float32)
    summed = onehot + weight_prior
    return summed / jnp.sum(summed, axis=0, keepdims=True)

def solve_normal(factor, right_sides):
    middle = lax.linalg.triangular_solve(factor, right_sides.T, left_side=True, lower=True)
    return lax.linalg.triangular_solve(factor, middle, left_side=True, lower=True, transpose_a=True)

def reference(animated, rest_positions, labels, weight_prior):
    highest = lax.Precision.HIGHEST
    homogeneous = jnp.concatenate([rest_positions, jnp.ones((1, VERTS), jnp.float32)], 0)
    weights = start_weights(labels, weight_prior)
    features = bone_features(weights, homogeneous)
    joint = 4 * B
    gram_matrix = lax.dot_general(features, features, (((1,), (1,)), ((), ())), precision=highest)
    gram_matrix = gram_matrix + ridge_scale * VERTS * jnp.eye(joint, dtype=jnp.float32)
    factor = jnp.linalg.cholesky(gram_matrix)
    blocks = animated.reshape(N_FRAME, 3 * FR_DEV, VERTS)

    def block(carry, rows):
        right_sides = lax.dot_general(rows, features, (((1,), (1,)), ((), ())), precision=highest)
        transforms = solve_normal(factor, right_sides)
        predicted = lax.dot_general(transforms, features, (((0,), (0,)), ((), ())), precision=highest)
        errors = rows - predicted
        pulled = jnp.dot(transforms, errors, precision=highest)
        return ((carry[0] + pulled, carry[1] + jnp.sum(errors * errors)), None)
    start = (jnp.zeros((joint, VERTS), jnp.float32), jnp.zeros((), jnp.float32))
    (pulled, squares), unused = lax.scan(block, start, blocks)
    gradient = -2.0 * jnp.sum(pulled.reshape(B, 4, VERTS) * homogeneous[None, :, :], axis=1)
    new_weights = jnp.clip(weights - step_size * gradient, 0.0, 1.0)
    fit_error = squares / (3.0 * FRAMES * VERTS)
    return (new_weights, fit_error)
```

```python
import functools
import jax
import jax.numpy as jnp
from jax import lax
from jax.experimental import pallas as pl
from jax.experimental.pallas import tpu as pltpu
from jax.sharding import PartitionSpec as P

HI = lax.Precision.HIGHEST
NT = (((1,), (1,)), ((), ()))
NN = (((1,), (0,)), ((), ()))
TN = (((0,), (0,)), ((), ()))

def make_weights(lab, prior):
    bones = prior.shape[0]
    ids = lax.broadcasted_iota(jnp.int32, prior.shape, 0)
    summed = jnp.where(ids == lab, 1.0, 0.0) + prior
    return summed / jnp.sum(summed, axis=0, keepdims=True)

def normal_kernel(n_chunk, anim, rest, lab, prior, d_out, w_out, rows, sem):
    n_rows, verts = anim.shape
    bones = prior.shape[0]
    cv = verts // n_chunk
    copies = []
    for j in range(n_chunk):
        cp = pltpu.make_async_copy(anim.at[:, pl.ds(j*cv, cv)], rows.at[:, pl.ds(j*cv, cv)], sem.at[j])
        cp.start()
        copies.append(cp)
    gram = jnp.zeros((4*bones, 4*bones), jnp.float32)
    rhs = jnp.zeros((n_rows, 4*bones), jnp.float32)
    for j in range(n_chunk):
        s = pl.ds(j*cv, cv)
        w = make_weights(lab[:, s], prior[:, s])
        w_out[:, s] = w
        f = jnp.concatenate([w * rest[k:k+1, s] for k in range(3)] + [w], axis=0)
        gram = gram + lax.dot_general(f, f, NT, precision=HI, preferred_element_type=jnp.float32)
        copies[j].wait()
        r = rows[:, s]
        rhs = rhs + lax.dot_general(r, f, NT, precision=HI, preferred_element_type=jnp.float32)
    lanes = 128
    g_tiles = gram.shape[0]//8
    for h in range(2):
        d_out[h*g_tiles:(h+1)*g_tiles] = gram[:, h*lanes:(h+1)*lanes].reshape(g_tiles, 8, lanes)
    r_tiles = rhs.shape[0]//8
    for h in range(2):
        d_out[2*g_tiles+h*r_tiles:2*g_tiles+(h+1)*r_tiles] = rhs[:, h*lanes:(h+1)*lanes].reshape(r_tiles, 8, lanes)

def normal(anim, rest, lab, prior, n_chunk=4):
    n_rows, verts = anim.shape
    bones = prior.shape[0]
    vm = pl.BlockSpec(memory_space=pltpu.VMEM)
    tiles = (4*bones + n_rows)*4*bones//1024
    return pl.pallas_call(
        functools.partial(normal_kernel, n_chunk),
        out_shape=(jax.ShapeDtypeStruct((tiles, 8, 128), jnp.float32), jax.ShapeDtypeStruct((bones, verts), jnp.float32)),
        in_specs=[pl.BlockSpec(memory_space=pltpu.HBM), vm, vm, vm],
        out_specs=(vm, vm),
        scratch_shapes=[pltpu.VMEM((n_rows, verts), jnp.float32), pltpu.SemaphoreType.DMA((n_chunk,))],
        compiler_params=pltpu.CompilerParams(vmem_limit_bytes=40 << 20),
    )(anim, rest, lab.reshape(1, verts), prior)


NX, NY = 4, 8

def vert_id(x, y, core):
    return (x*NY + y)*2 + core

def remote(src, dst, s, r, peer, axis="vert"):
    return pltpu.make_async_remote_copy(src, dst, s, r, device_id={axis: peer}, device_id_type=pl.DeviceIdType.MESH)

def reduce_kernel(d, out, b0, acc, b1, sub, b2, gat, s0, r0, s1, r1, s2, r2, s3, r3, s4, r4, s5, r5):
    me = lax.axis_index("vert")
    core = lax.rem(me, 2)
    y = lax.rem(me//2, NY)
    x = me//(2*NY)
    sib = vert_id(x, y, 1-core)
    xs = [lax.rem(x+k, NX) for k in range(NX)]
    ys = [lax.rem(y+k, NY) for k in range(NY)]
    half = d.shape[0]//2
    q = half//NX
    e = gat.shape[0]//NY
    peers = [sib] + [vert_id(a, y, core) for a in xs[1:]] + [vert_id(x, a, core) for a in ys[1:]]
    barrier = pltpu.get_barrier_semaphore()
    for p in peers:
        pl.semaphore_signal(barrier, inc=1, device_id={"vert": p}, device_id_type=pl.DeviceIdType.MESH)
    pl.semaphore_wait(barrier, len(peers))
    order = (2, 1, 3, 0)
    c0 = []
    for i, k in enumerate(order):
        cp = remote(d.at[pl.ds((1-core)*half + xs[k]*q, q)], b0.at[i], s0.at[i], r0.at[i], sib)
        cp.start()
        c0.append(cp)
    c1 = {}
    for i, k in enumerate(order):
        c0[i].wait_recv()
        acc[i] = b0[i] + d[pl.ds(core*half + xs[k]*q, q)]
        if k:
            c1[k] = remote(acc.at[i], b1.at[k-1], s1.at[k-1], r1.at[k-1], vert_id(xs[k], y, core))
            c1[k].start()
    tot = acc[3]
    for k in (1, 3, 2):
        c1[k].wait_recv()
        tot = tot + b1[k-1]
    sub[0:q] = tot
    sub[q:] = jnp.zeros((sub.shape[0]-q, 8, 128), jnp.float32)
    c2 = {}
    yorder = (4, 3, 5, 2, 6, 1, 7)
    for k in yorder:
        c2[k] = remote(sub.at[pl.ds(ys[k]*e, e)], b2.at[k-1], s2.at[k-1], r2.at[k-1], vert_id(x, ys[k], core))
        c2[k].start()
    tot = sub[pl.ds(y*e, e)]
    for k in yorder[::-1]:
        c2[k].wait_recv()
        tot = tot + b2[k-1]
    gat[pl.ds(y*e, e)] = tot
    c3 = {}
    for k in yorder:
        c3[k] = remote(gat.at[pl.ds(y*e, e)], gat.at[pl.ds(y*e, e)], s3.at[k-1], r3.at[k-1], vert_id(x, ys[k], core))
        c3[k].start()
    for k in yorder[::-1]:
        c3[k].wait_recv()
    mine = pl.ds(core*half + x*q, q)
    out[mine] = gat[0:q]
    c4 = {}
    for k in (2, 1, 3):
        c4[k] = remote(out.at[mine], out.at[mine], s4.at[k-1], r4.at[k-1], vert_id(xs[k], y, core))
        c4[k].start()
    c5 = []
    for i, k in enumerate((0, 1, 3, 2)):
        if k:
            c4[k].wait_recv()
        blk = pl.ds(core*half + lax.rem(x + NX - k, NX)*q, q)
        cp = remote(out.at[blk], out.at[blk], s5.at[i], r5.at[i], sib)
        cp.start()
        c5.append(cp)
    for cp in c5:
        cp.wait_recv()
    for cp in c0 + list(c1.values()) + list(c2.values()) + list(c3.values()) + list(c4.values()) + c5:
        cp.wait_send()

def reduce_vert(d):
    tiles = d.shape[0]
    half = tiles//2
    q = half//NX
    e = -(-q//NY)
    vm = pl.BlockSpec(memory_space=pltpu.VMEM)
    buf = lambda *s: pltpu.VMEM(s + (8, 128), jnp.float32)
    sems = lambda n: [pltpu.SemaphoreType.DMA((n,))]*2
    return pl.pallas_call(
        reduce_kernel, out_shape=jax.ShapeDtypeStruct(d.shape, d.dtype), in_specs=[vm], out_specs=vm,
        scratch_shapes=[buf(NX, q), buf(NX, q), buf(NX-1, q), buf(NY*e), buf(NY-1, e), buf(NY*e)]
        + sems(4) + sems(3) + sems(7) + sems(7) + sems(3) + sems(4),
        compiler_params=pltpu.CompilerParams(collective_id=0, has_side_effects=True, vmem_limit_bytes=24 << 20),
        name="reduce_vert",
    )(d)


ridge_scale = 0.0001
step_size = 0.005

def hdot(a, b, dims=NN):
    return lax.dot_general(a, b, dims, precision=HI, preferred_element_type=jnp.float32)

def sweep_small(p):
    n = p.shape[0]
    sub = lax.broadcasted_iota(jnp.int32, (n, 1), 0)
    lane = lax.broadcasted_iota(jnp.int32, (1, n), 1)
    for k in range(n):
        row, col = p[k:k+1, :], p[:, k:k+1]
        inv = 1.0/p[k:k+1, k:k+1]
        colp = jnp.where(sub == k, -1.0, col)
        wp = jnp.where(lane == k, -1.0, row)*inv
        p = jnp.where((sub == k) | (lane == k), 0.0, p) - colp*wp
    return p

def negative_inverse(a, nb=32):
    n = a.shape[0]
    sub = lax.broadcasted_iota(jnp.int32, (n, n), 0)//nb
    lane = lax.broadcasted_iota(jnp.int32, (n, n), 1)//nb
    eye = (lax.broadcasted_iota(jnp.int32, (nb, nb), 0) == lax.broadcasted_iota(jnp.int32, (nb, nb), 1)).astype(jnp.float32)
    for i in range(n//nb):
        s = i*nb
        rows = a[s:s+nb]
        neg = sweep_small(rows[:, s:s+nb])
        w = -hdot(neg, rows)
        parts = lambda mid, full: jnp.concatenate(([full[:, :s]] if s else []) + [mid] + ([full[:, s+nb:]] if s+nb < n else []), axis=1)
        a = jnp.where((sub == i) | (lane == i), 0.0, a) - hdot(parts(-eye, rows), parts(neg, w), TN)
    return a

def fit_kernel(n_chunk, ridge, anim, d, rest, w_ref, g_out, e_out, rows, sem):
    n_rows, verts = anim.shape
    bones = w_ref.shape[0]
    joint = 4*bones
    cv = verts // n_chunk
    copies = []
    for j in range(n_chunk):
        cp = pltpu.make_async_copy(anim.at[:, pl.ds(j*cv, cv)], rows.at[:, pl.ds(j*cv, cv)], sem.at[j])
        cp.start()
        copies.append(cp)
    gt, rt = joint//8, n_rows//8
    eye = lax.broadcasted_iota(jnp.int32, (joint, joint), 0) == lax.broadcasted_iota(jnp.int32, (joint, joint), 1)
    gram = jnp.concatenate([d[h*gt:(h+1)*gt].reshape(joint, 128) for h in range(2)], axis=1)
    gram = gram + jnp.where(eye, ridge, 0.0)
    rhs = jnp.concatenate([d[2*gt+h*rt:2*gt+(h+1)*rt].reshape(n_rows, 128) for h in range(2)], axis=1)
    neg = negative_inverse(gram)
    tt = -hdot(rhs, neg)
    tt = tt - hdot(rhs - hdot(tt, gram), neg)
    t = tt.T
    total = jnp.zeros((8, 128), jnp.float32)
    for j in range(n_chunk):
        s = pl.ds(j*cv, cv)
        w = w_ref[:, s]
        h = [rest[k:k+1, s] for k in range(3)]
        f = jnp.concatenate([w * h[k] for k in range(3)] + [w], axis=0)
        copies[j].wait()
        r = rows[:, s]
        e = r - hdot(tt, f)
        sq = (e*e).reshape(n_rows//8, 8, cv).sum(axis=0)
        for q in range(cv//128):
            total = total + sq[:, q*128:(q+1)*128]
        pulled = hdot(t, e)
        grad = pulled[3*bones:]
        for k in range(3):
            grad = grad + pulled[k*bones:(k+1)*bones]*h[k]
        g_out[:, :, s] = (-2.0*grad).reshape(bones//8, 8, cv)
    e_out[0] = total

def fit(anim, d, rest, w, verts_total, n_chunk=4):
    n_rows, verts = anim.shape
    bones = w.shape[0]
    vm = pl.BlockSpec(memory_space=pltpu.VMEM)
    return pl.pallas_call(
        functools.partial(fit_kernel, n_chunk, ridge_scale*verts_total),
        out_shape=(jax.ShapeDtypeStruct((bones//8, 8, verts), jnp.float32), jax.ShapeDtypeStruct((1, 8, 128), jnp.float32)),
        in_specs=[pl.BlockSpec(memory_space=pltpu.HBM), vm, vm, vm],
        out_specs=(vm, vm),
        scratch_shapes=[pltpu.VMEM((n_rows, verts), jnp.float32), pltpu.SemaphoreType.DMA((n_chunk,))],
        compiler_params=pltpu.CompilerParams(vmem_limit_bytes=40 << 20),
        name="fit",
    )(anim, d, rest, w)


def frame_kernel(scale, g, e, w, out, f_out, gb, ez, ey, ex, ec, et, sg, rg, sa, ra, sz, rz, sy, ry, sx, rx, sc, rc):
    me = lax.axis_index("vert")
    z = lax.axis_index("frame")
    nz = g.shape[0]
    core = lax.rem(me, 2)
    y = lax.rem(me//2, NY)
    x = me//(2*NY)
    sib = vert_id(x, y, 1-core)
    zs = [lax.rem(z+k, nz) for k in range(nz)]
    xs = [vert_id(lax.rem(x+k, NX), y, core) for k in range(NX)]
    ys = [vert_id(x, lax.rem(y+k, NY), core) for k in range(NY)]
    barrier = pltpu.get_barrier_semaphore()
    for p in [sib] + xs[1:] + ys[1:]:
        pl.semaphore_signal(barrier, inc=1, device_id={"vert": p}, device_id_type=pl.DeviceIdType.MESH)
    for p in zs[1:]:
        pl.semaphore_signal(barrier, inc=1, device_id={"frame": p}, device_id_type=pl.DeviceIdType.MESH)
    pl.semaphore_wait(barrier, 1 + NX-1 + NY-1 + nz-1)
    order = (4, 3, 5, 2, 6, 1, 7)
    cz = [remote(e.at[0], ez.at[k-1], sz.at[k-1], rz.at[k-1], zs[k], "frame") for k in order]
    for cp in cz:
        cp.start()
    cg = [remote(g.at[zs[k]], gb.at[k-1], sg.at[k-1], rg.at[k-1], zs[k], "frame") for k in order]
    for cp in cg:
        cp.start()
    for cp in cz:
        cp.wait_recv()
    tot = e[0]
    for k in range(1, nz):
        tot = tot + ez[k-1]
    et[0] = tot
    cy = [remote(et.at[0], ey.at[k-1], sy.at[k-1], ry.at[k-1], ys[k]) for k in order]
    for cp in cy:
        cp.start()
    for cp in cy:
        cp.wait_recv()
    tot = et[0]
    for k in range(1, NY):
        tot = tot + ey[k-1]
    et[1] = tot
    cx = [remote(et.at[1], ex.at[k-1], sx.at[k-1], rx.at[k-1], xs[k]) for k in (2, 1, 3)]
    for cp in cx:
        cp.start()
    for cp in cx:
        cp.wait_recv()
    tot = et[1]
    for k in range(1, NX):
        tot = tot + ex[k-1]
    et[2] = tot
    cc = remote(et.at[2], ec.at[0], sc.at[0], rc.at[0], sib)
    cc.start()
    grad = g[z]
    for cp, k in zip(cg[::-1], order[::-1]):
        cp.wait_recv()
        grad = grad + gb[k-1]
    out[z] = jnp.clip(w[z] - step_size*grad, 0.0, 1.0)
    ca = [remote(out.at[z], out.at[z], sa.at[k-1], ra.at[k-1], zs[k], "frame") for k in order]
    for cp in ca:
        cp.start()
    cc.wait_recv()
    f_out[...] = jnp.sum(et[2] + ec[0], axis=(0, 1), keepdims=True)*scale
    for cp in ca:
        cp.wait_recv()
    for cp in cz + cg + cy + cx + [cc] + ca:
        cp.wait_send()

def reduce_frame(g, e, w, scale):
    nz, eight, verts = g.shape
    vm = pl.BlockSpec(memory_space=pltpu.VMEM)
    buf = lambda *s: pltpu.VMEM(s + (8, 128), jnp.float32)
    sems = lambda n: [pltpu.SemaphoreType.DMA((n,))]*2
    return pl.pallas_call(
        functools.partial(frame_kernel, scale),
        out_shape=(jax.ShapeDtypeStruct(g.shape, g.dtype), jax.ShapeDtypeStruct((1, 1), jnp.float32)),
        in_specs=[vm, vm, vm], out_specs=(vm, vm),
        scratch_shapes=[pltpu.VMEM((nz-1, eight, verts), jnp.float32), buf(nz-1), buf(NY-1), buf(NX-1), buf(1), buf(3)]
        + sems(nz-1) + sems(nz-1) + sems(nz-1) + sems(NY-1) + sems(NX-1) + sems(1),
        compiler_params=pltpu.CompilerParams(collective_id=1, has_side_effects=True, vmem_limit_bytes=24 << 20),
        name="reduce_frame",
    )(g, e, w)


def local(animated, rest_positions, labels, weight_prior):
    bones, local_verts = weight_prior.shape
    verts_total = local_verts * lax.axis_size("vert")
    frames_total = animated.shape[0] * lax.axis_size("frame")
    rows = animated.transpose(1, 0, 2).reshape(-1, local_verts)
    sums, weights = normal(rows, rest_positions, labels, weight_prior)
    sums = reduce_vert(sums)
    grad, squares = fit(rows, sums, rest_positions, weights, verts_total)
    scale = 1.0 / (3.0 * frames_total * verts_total)
    new_weights, fit_error = reduce_frame(grad, squares, weights.reshape(grad.shape), scale)
    return new_weights.reshape(bones, local_verts), fit_error.reshape(())


def solution(mesh):
    placed = (P("frame", None, "vert"), P(None, "vert"), P("vert"), P(None, "vert"))
    return jax.shard_map(
        local, mesh=mesh, in_specs=placed, out_specs=(P(None, "vert"), P()), check_vma=False
    )
```

```python
import functools

import jax
import jax.numpy as jnp
from jax import lax
from jax.experimental import pallas as pl
from jax.experimental.pallas import tpu as pltpu
from jax.sharding import PartitionSpec as P

HI = lax.Precision.HIGHEST
MESH = pl.DeviceIdType.MESH
NT = (((1,), (1,)), ((), ()))
NN = (((1,), (0,)), ((), ()))
TN = (((0,), (0,)), ((), ()))
NX, NY, NZ = 4, 8, 8
CHUNKS = 4
ridge_scale = 0.0001
step_size = 0.005
far_first = (4, 3, 5, 2, 6, 1, 7)


def hdot(a, b, dims=NN):
    return lax.dot_general(a, b, dims, precision=HI, preferred_element_type=jnp.float32)


def sym(f, n):
    m = [[None] * n for _ in range(n)]
    for i in range(n):
        for j in range(i, n):
            m[i][j] = m[j][i] = f(i, j)
    return m


def total(terms):
    while len(terms) > 1:
        terms = [terms[i] + terms[i + 1] for i in range(0, len(terms) - 1, 2)] + (
            [terms[-1]] if len(terms) % 2 else []
        )
    return terms[0]


def inv_sym(m):
    n = len(m)
    if n == 2:
        r = 1.0 / (m[0][0] * m[1][1] - m[0][1] * m[0][1])
        b = -m[0][1] * r
        return [[m[1][1] * r, b], [b, m[0][0] * r]]
    h = n // 2
    rng = range(h)
    a = inv_sym([row[:h] for row in m[:h]])
    f = [row[h:] for row in m[:h]]
    af = [[total([a[i][l] * f[l][j] for l in rng]) for j in rng] for i in rng]
    s = inv_sym(sym(lambda i, j: m[h + i][h + j] - total([f[l][i] * af[l][j] for l in rng]), h))
    off = [[-total([af[i][l] * s[l][j] for l in rng]) for j in rng] for i in rng]
    top = sym(lambda i, j: a[i][j] - total([off[i][l] * af[j][l] for l in rng]), h)
    return [top[i] + off[i] for i in rng] + [[off[j][i] for j in rng] + s[i] for i in rng]


def sweep(p, b):
    n = p.shape[0]
    sub = lax.broadcasted_iota(jnp.int32, (n, n), 0)
    lane = lax.broadcasted_iota(jnp.int32, (n, n), 1)
    lane1 = lane[0:1]
    for k in range(0, n, b):
        c = [jnp.broadcast_to(p[:, k + j : k + j + 1], (n, n)) for j in range(b)]
        m = inv_sym(sym(lambda i, j: c[j][k + i : k + i + 1], b))
        r = [
            jnp.where(lane1 == k + j, -1.0, jnp.where(lane1 // b == k // b, 0.0, p[k + j : k + j + 1]))
            for j in range(b)
        ]
        w = [total([m[i][j] * r[j] for j in range(b)]) for i in range(b)]
        c = [jnp.where(sub == k + j, -1.0, jnp.where(sub // b == k // b, 0.0, c[j])) for j in range(b)]
        keep = jnp.where((sub // b == k // b) | (lane // b == k // b), 0.0, p)
        p = keep - total([c[j] * w[j] for j in range(b)])
    return p


def negative_inverse(a, nb, b, between):
    n = a.shape[0]
    sub = lax.broadcasted_iota(jnp.int32, (n, n), 0) // nb
    lane = lax.broadcasted_iota(jnp.int32, (n, n), 1) // nb
    square = (nb, nb)
    eye = (
        lax.broadcasted_iota(jnp.int32, square, 0) == lax.broadcasted_iota(jnp.int32, square, 1)
    ).astype(jnp.float32)
    for i in range(n // nb):
        s = i * nb
        rows = a[s : s + nb]
        neg = sweep(rows[:, s : s + nb], b)
        w = -hdot(neg, rows)

        def parts(middle, full):
            left = [full[:, :s]] if s else []
            right = [full[:, s + nb :]] if s + nb < n else []
            return jnp.concatenate(left + [middle] + right, axis=1)

        a = jnp.where((sub == i) | (lane == i), 0.0, a) - hdot(parts(-eye, rows), parts(neg, w), TN)
        between(i)
    return a


class Place:
    def __init__(self):
        me = lax.axis_index("vert")
        self.core = lax.rem(me, 2)
        self.y = lax.rem(me // 2, NY)
        self.x = me // (2 * NY)
        self.z = lax.axis_index("frame")
        self.xs = [lax.rem(self.x + k, NX) for k in range(NX)]
        self.ys = [lax.rem(self.y + k, NY) for k in range(NY)]
        self.zs = [lax.rem(self.z + k, NZ) for k in range(NZ)]
        vert = lambda x, y, core: {"vert": (x * NY + y) * 2 + core}
        self.sib = vert(self.x, self.y, 1 - self.core)
        self.xp = [vert(a, self.y, self.core) for a in self.xs]
        self.yp = [vert(self.x, a, self.core) for a in self.ys]
        self.zp = [{"frame": a} for a in self.zs]


def send(src, dst, s, r, peer):
    cp = pltpu.make_async_remote_copy(src, dst, s, r, device_id=peer, device_id_type=MESH)
    cp.start()
    return cp


def reduce_steps(pos, d, bufs, sems, sent):
    b0, acc, b1, sub, b2, gat, full = bufs
    (s0, r0), (s1, r1), (s2, r2), (s3, r3), (s4, r4), (s5, r5) = sems
    half = d.shape[0] // 2
    q = half // NX
    e = gat.shape[0] // NY
    xs, ys, core = pos.xs, pos.ys, pos.core
    order = (2, 1, 3, 0)
    c0 = [
        send(d.at[pl.ds((1 - core) * half + xs[k] * q, q)], b0.at[i], s0.at[i], r0.at[i], pos.sib)
        for i, k in enumerate(order)
    ]
    sent += c0
    yield
    c1 = {}
    for i, k in enumerate(order):
        c0[i].wait_recv()
        acc[i] = b0[i] + d[pl.ds(core * half + xs[k] * q, q)]
        if k:
            c1[k] = send(acc.at[i], b1.at[k - 1], s1.at[k - 1], r1.at[k - 1], pos.xp[k])
    sent += c1.values()
    yield
    tot = acc[3]
    for k in (1, 3, 2):
        c1[k].wait_recv()
        tot = tot + b1[k - 1]
    sub[0:q] = tot
    if NY * e > q:
        sub[q:] = jnp.zeros((NY * e - q, 8, 128), jnp.float32)
    c2 = {
        k: send(sub.at[pl.ds(ys[k] * e, e)], b2.at[k - 1], s2.at[k - 1], r2.at[k - 1], pos.yp[k])
        for k in far_first
    }
    sent += c2.values()
    yield
    mine = pl.ds(pos.y * e, e)
    tot = sub[mine]
    for k in far_first[::-1]:
        c2[k].wait_recv()
        tot = tot + b2[k - 1]
    gat[mine] = tot
    c3 = {
        k: send(gat.at[mine], gat.at[mine], s3.at[k - 1], r3.at[k - 1], pos.yp[k]) for k in far_first
    }
    sent += c3.values()
    yield
    for k in far_first[::-1]:
        c3[k].wait_recv()
    mine = pl.ds(core * half + pos.x * q, q)
    full[mine] = gat[0:q]
    c4 = {k: send(full.at[mine], full.at[mine], s4.at[k - 1], r4.at[k - 1], pos.xp[k]) for k in (2, 1, 3)}
    c5 = [send(full.at[mine], full.at[mine], s5.at[0], r5.at[0], pos.sib)]
    sent += c4.values()
    yield
    for i, k in enumerate((1, 3, 2)):
        c4[k].wait_recv()
        blk = pl.ds(core * half + lax.rem(pos.x + NX - k, NX) * q, q)
        c5.append(send(full.at[blk], full.at[blk], s5.at[i + 1], r5.at[i + 1], pos.sib))
    sent += c5
    yield
    for cp in c5:
        cp.wait_recv()
    yield


def kernel(ridge, scale, *refs):
    it = iter(refs)
    take = lambda n: [next(it) for _ in range(n)]
    anim, rest_h, lab_h, prior_h, out, f_out = take(6)
    rows, feats, rest, lab, w_ref, dg, dr, g, gb = take(9)
    ez, ey, ex, ec, et = take(5)
    g_bufs, r_bufs = take(7), take(7)
    in_sem, row_sem = take(2)
    pairs = lambda n: [tuple(take(2)) for _ in range(n)]
    g_sems, r_sems = pairs(6), pairs(6)
    (sg, rg), (sa, ra), (sz, rz), (sy, ry), (sx, rx), (sc, rc) = pairs(6)

    n_rows, verts = anim.shape
    bones = prior_h.shape[0]
    joint = 4 * bones
    cv = verts // CHUNKS
    pos = Place()

    small = [
        pltpu.make_async_copy(src, dst, in_sem.at[i])
        for i, (src, dst) in enumerate(((prior_h, w_ref), (rest_h, rest), (lab_h, lab)))
    ]
    for cp in small:
        cp.start()
    for j in range(CHUNKS):
        s = pl.ds(j * cv, cv)
        pltpu.make_async_copy(anim.at[:, s], rows.at[:, s], row_sem.at[j]).start()
    barrier = pltpu.get_barrier_semaphore()
    peers = [pos.sib] + pos.xp[1:] + pos.yp[1:] + pos.zp[1:]
    for p in peers:
        pl.semaphore_signal(barrier, inc=1, device_id=p, device_id_type=MESH)
    for cp in small:
        cp.wait()

    ids = lax.broadcasted_iota(jnp.int32, (bones, cv), 0)

    def gram_chunk(j, gram):
        s = pl.ds(pl.multiple_of(j * cv, cv), cv)
        summed = jnp.where(ids == lab[:, s], 1.0, 0.0) + w_ref[:, s]
        w = summed / jnp.sum(summed, axis=0, keepdims=True)
        w_ref[:, s] = w
        f = jnp.concatenate([w * rest[k : k + 1, s] for k in range(3)] + [w], axis=0)
        feats[:, s] = f
        return gram + hdot(f, f, NT)

    gram = lax.fori_loop(0, CHUNKS, gram_chunk, jnp.zeros((joint, joint), jnp.float32))
    gt, rt = joint // 8, n_rows // 8
    for h in range(2):
        dg[h * gt : (h + 1) * gt] = gram[:, h * 128 : (h + 1) * 128].reshape(gt, 8, 128)
    sent = []
    pl.semaphore_wait(barrier, len(peers))
    gsteps = reduce_steps(pos, dg, g_bufs, g_sems, sent)
    rsteps = reduce_steps(pos, dr, r_bufs, r_sems, sent)
    next(gsteps)

    def rhs_chunk(j, rhs):
        s = pl.ds(pl.multiple_of(j * cv, cv), cv)
        pltpu.make_async_copy(anim.at[:, s], rows.at[:, s], row_sem.at[j]).wait()
        return rhs + hdot(rows[:, s], feats[:, s], NT)

    next(gsteps)
    rhs = lax.fori_loop(0, CHUNKS, rhs_chunk, jnp.zeros((n_rows, joint), jnp.float32))
    for h in range(2):
        dr[h * rt : (h + 1) * rt] = rhs[:, h * 128 : (h + 1) * 128].reshape(rt, 8, 128)
    next(rsteps)
    next(gsteps)
    next(rsteps)
    next(gsteps)
    next(rsteps)
    next(gsteps)
    next(rsteps)
    next(gsteps)
    next(gsteps)

    square = (joint, joint)
    eye = lax.broadcasted_iota(jnp.int32, square, 0) == lax.broadcasted_iota(jnp.int32, square, 1)
    dg, dr = g_bufs[-1], r_bufs[-1]
    gram = jnp.concatenate([dg[h * gt : (h + 1) * gt].reshape(joint, 128) for h in range(2)], axis=1)
    gram = gram + jnp.where(eye, ridge, 0.0)
    neg = negative_inverse(gram, 64, 4, lambda i: next(rsteps) if i < 3 else None)
    rhs = jnp.concatenate([dr[h * rt : (h + 1) * rt].reshape(n_rows, 128) for h in range(2)], axis=1)
    tt = -hdot(rhs, neg)
    tt = tt - hdot(rhs - hdot(tt, gram), neg)
    t = tt.T

    def fit_chunk(j, squares):
        s = pl.ds(pl.multiple_of(j * cv, cv), cv)
        e = rows[:, s] - hdot(tt, feats[:, s])
        pulled = hdot(t, e)
        grad = pulled[3 * bones :]
        for k in range(3):
            grad = grad + pulled[k * bones : (k + 1) * bones] * rest[k : k + 1, s]
        g[:, :, s] = (-2.0 * grad).reshape(NZ, bones // NZ, cv)
        for k in far_first:
            send(g.at[pos.zs[k], :, s], gb.at[k - 1, :, s], sg.at[j, k - 1], rg.at[j, k - 1], pos.zp[k])
        sq = (e * e).reshape(n_rows // 8, 8, cv).sum(axis=0)
        return squares + total([sq[:, i * 128 : (i + 1) * 128] for i in range(cv // 128)])

    et[0] = lax.fori_loop(0, CHUNKS, fit_chunk, jnp.zeros((8, 128), jnp.float32))
    cz = [send(et.at[0], ez.at[k - 1], sz.at[k - 1], rz.at[k - 1], pos.zp[k]) for k in far_first]

    mine = pl.ds(pl.multiple_of(pos.z * (bones // NZ), bones // NZ), bones // NZ)

    def update_chunk(j, carry):
        s = pl.ds(pl.multiple_of(j * cv, cv), cv)
        grad = g[pos.z, :, s]
        for k in far_first[::-1]:
            pltpu.make_async_remote_copy(
                g.at[pos.zs[k], :, s], gb.at[k - 1, :, s], sg.at[j, k - 1], rg.at[j, k - 1],
                device_id=pos.zp[k], device_id_type=MESH,
            ).wait()
            grad = grad + gb[k - 1, :, s]
        out[pos.z, :, s] = jnp.clip(w_ref[mine, s] - step_size * grad, 0.0, 1.0)
        for k in far_first:
            send(out.at[pos.z, :, s], out.at[pos.z, :, s], sa.at[j, k - 1], ra.at[j, k - 1], pos.zp[k])
        return carry

    lax.fori_loop(0, CHUNKS, update_chunk, 0)

    def add_up(copies, buf, i):
        tot = et[i]
        for cp in copies:
            cp.wait_recv()
        for k in range(buf.shape[0]):
            tot = tot + buf[k]
        et[i + 1] = tot

    add_up(cz, ez, 0)
    cy = [send(et.at[1], ey.at[k - 1], sy.at[k - 1], ry.at[k - 1], pos.yp[k]) for k in far_first]
    add_up(cy, ey, 1)
    cx = [send(et.at[2], ex.at[k - 1], sx.at[k - 1], rx.at[k - 1], pos.xp[k]) for k in (2, 1, 3)]
    add_up(cx, ex, 2)
    cc = [send(et.at[3], ec.at[0], sc.at[0], rc.at[0], pos.sib)]
    add_up(cc, ec, 3)
    f_out[...] = jnp.sum(et[4], axis=(0, 1), keepdims=True) * scale

    def gather_chunk(j, carry):
        s = pl.ds(pl.multiple_of(j * cv, cv), cv)
        for k in far_first[::-1]:
            pltpu.make_async_remote_copy(
                out.at[pos.z, :, s], out.at[pos.z, :, s], sa.at[j, k - 1], ra.at[j, k - 1],
                device_id=pos.zp[k], device_id_type=MESH,
            ).wait()
        return carry

    lax.fori_loop(0, CHUNKS, gather_chunk, 0)
    for cp in sent + cz + cy + cx + cc:
        cp.wait_send()


def local(animated, rest_positions, labels, weight_prior):
    bones, verts = weight_prior.shape
    n_rows = 3 * animated.shape[0]
    joint = 4 * bones
    verts_total = verts * lax.axis_size("vert")
    frames_total = animated.shape[0] * lax.axis_size("frame")
    rows = animated.transpose(1, 0, 2).reshape(n_rows, verts)

    vmem = lambda *s: pltpu.VMEM(s, jnp.float32)
    tiles = lambda *s: vmem(*s, 8, 128)

    def buffers(n):
        q = n // (2 * NX)
        e = -(-q // NY)
        return [tiles(NX, q), tiles(NX, q), tiles(NX - 1, q), tiles(NY * e), tiles(NY - 1, e), tiles(NY * e), tiles(n)]

    pair = lambda *s: [pltpu.SemaphoreType.DMA(s)] * 2
    reduce_pairs = pair(4) + pair(3) + pair(7) + pair(7) + pair(3) + pair(4)
    n_gram, n_rhs = joint * joint // 1024, n_rows * joint // 1024
    scratch = [
        vmem(n_rows, verts), vmem(joint, verts), vmem(3, verts), pltpu.VMEM((1, verts), jnp.int32),
        vmem(bones, verts), tiles(n_gram), tiles(n_rhs), vmem(NZ, bones // NZ, verts),
        vmem(NZ - 1, bones // NZ, verts), tiles(NZ - 1), tiles(NY - 1), tiles(NX - 1), tiles(1), tiles(5),
    ]
    scratch += buffers(n_gram) + buffers(n_rhs)
    scratch += [pltpu.SemaphoreType.DMA((3,)), pltpu.SemaphoreType.DMA((CHUNKS,))]
    scratch += reduce_pairs + reduce_pairs
    scratch += pair(CHUNKS, NZ - 1) + pair(CHUNKS, NZ - 1) + pair(NZ - 1) + pair(NY - 1) + pair(NX - 1) + pair(1)

    hbm, vm = pl.BlockSpec(memory_space=pltpu.HBM), pl.BlockSpec(memory_space=pltpu.VMEM)
    new_weights, fit_error = pl.pallas_call(
        functools.partial(kernel, ridge_scale * verts_total, 1.0 / (3.0 * frames_total * verts_total)),
        out_shape=(
            jax.ShapeDtypeStruct((NZ, bones // NZ, verts), jnp.float32),
            jax.ShapeDtypeStruct((1, 1), jnp.float32),
        ),
        in_specs=[hbm] * 4,
        out_specs=(vm, vm),
        scratch_shapes=scratch,
        compiler_params=pltpu.CompilerParams(
            collective_id=0, has_side_effects=True, vmem_limit_bytes=56 << 20
        ),
        name="skinning",
    )(rows, rest_positions, labels.reshape(1, verts), weight_prior)
    return new_weights.reshape(bones, verts), fit_error.reshape(())


def solution(mesh):
    placed = (P("frame", None, "vert"), P(None, "vert"), P("vert"), P(None, "vert"))
    return jax.shard_map(
        local, mesh=mesh, in_specs=placed, out_specs=(P(None, "vert"), P()), check_vma=False
    )
```

```python
import functools

import jax
import jax.numpy as jnp
from jax import lax
from jax.experimental import pallas as pl
from jax.experimental.pallas import tpu as pltpu
from jax.sharding import PartitionSpec as P

HI = lax.Precision.HIGHEST
MESH = pl.DeviceIdType.MESH
NT = (((1,), (1,)), ((), ()))
NN = (((1,), (0,)), ((), ()))
TN = (((0,), (0,)), ((), ()))
NX, NY, NZ = 4, 8, 8
CHUNKS = 4
ridge_scale = 0.0001
step_size = 0.005
far_first = (4, 3, 5, 2, 6, 1, 7)


def hdot(a, b, dims=NN):
    return lax.dot_general(a, b, dims, precision=HI, preferred_element_type=jnp.float32)


def halves(a):
    high = a.astype(jnp.bfloat16)
    return high, (a - high.astype(jnp.float32)).astype(jnp.bfloat16)


def dot3(a, b):
    dot = lambda x, y: lax.dot_general(x, y, NN, preferred_element_type=jnp.float32)
    return dot(a[0], b[0]) + (dot(a[0], b[1]) + dot(a[1], b[0]))


def sym(f, n):
    m = [[None] * n for _ in range(n)]
    for i in range(n):
        for j in range(i, n):
            m[i][j] = m[j][i] = f(i, j)
    return m


def total(terms):
    while len(terms) > 1:
        terms = [terms[i] + terms[i + 1] for i in range(0, len(terms) - 1, 2)] + (
            [terms[-1]] if len(terms) % 2 else []
        )
    return terms[0]


def inv_sym(m):
    n = len(m)
    if n == 2:
        r = 1.0 / (m[0][0] * m[1][1] - m[0][1] * m[0][1])
        b = -m[0][1] * r
        return [[m[1][1] * r, b], [b, m[0][0] * r]]
    h = n // 2
    rng = range(h)
    a = inv_sym([row[:h] for row in m[:h]])
    f = [row[h:] for row in m[:h]]
    af = [[total([a[i][l] * f[l][j] for l in rng]) for j in rng] for i in rng]
    s = inv_sym(sym(lambda i, j: m[h + i][h + j] - total([f[l][i] * af[l][j] for l in rng]), h))
    off = [[-total([af[i][l] * s[l][j] for l in rng]) for j in rng] for i in rng]
    top = sym(lambda i, j: a[i][j] - total([off[i][l] * af[j][l] for l in rng]), h)
    return [top[i] + off[i] for i in rng] + [[off[j][i] for j in rng] + s[i] for i in rng]


def sweep(p, b, halfway):
    n = p.shape[0]
    sub = lax.broadcasted_iota(jnp.int32, (n, n), 0)
    lane = lax.broadcasted_iota(jnp.int32, (n, n), 1)
    lane1 = lane[0:1]
    for k in range(0, n, b):
        if k == n // 2:
            halfway()
        c = [jnp.broadcast_to(p[:, k + j : k + j + 1], (n, n)) for j in range(b)]
        m = inv_sym(sym(lambda i, j: c[j][k + i : k + i + 1], b))
        r = [
            jnp.where(lane1 == k + j, -1.0, jnp.where(lane1 // b == k // b, 0.0, p[k + j : k + j + 1]))
            for j in range(b)
        ]
        w = [total([m[i][j] * r[j] for j in range(b)]) for i in range(b)]
        c = [jnp.where(sub == k + j, -1.0, jnp.where(sub // b == k // b, 0.0, c[j])) for j in range(b)]
        keep = jnp.where((sub // b == k // b) | (lane // b == k // b), 0.0, p)
        p = keep - total([c[j] * w[j] for j in range(b)])
    return p


def negative_inverse(a, nb, b, between):
    n = a.shape[0]
    sub = lax.broadcasted_iota(jnp.int32, (n, n), 0) // nb
    lane = lax.broadcasted_iota(jnp.int32, (n, n), 1) // nb
    square = (nb, nb)
    eye = (
        lax.broadcasted_iota(jnp.int32, square, 0) == lax.broadcasted_iota(jnp.int32, square, 1)
    ).astype(jnp.float32)
    for i in range(n // nb):
        s = i * nb
        rows = a[s : s + nb]
        neg = sweep(rows[:, s : s + nb], b, lambda: between(2 * i))
        w = -hdot(neg, rows)

        def parts(middle, full):
            left = [full[:, :s]] if s else []
            right = [full[:, s + nb :]] if s + nb < n else []
            return jnp.concatenate(left + [middle] + right, axis=1)

        a = jnp.where((sub == i) | (lane == i), 0.0, a) - hdot(parts(-eye, rows), parts(neg, w), TN)
        between(2 * i + 1)
    return a


class Place:
    def __init__(self):
        me = lax.axis_index("vert")
        self.core = lax.rem(me, 2)
        self.y = lax.rem(me // 2, NY)
        self.x = me // (2 * NY)
        self.z = lax.axis_index("frame")
        self.xs = [lax.rem(self.x + k, NX) for k in range(NX)]
        self.ys = [lax.rem(self.y + k, NY) for k in range(NY)]
        self.zs = [lax.rem(self.z + k, NZ) for k in range(NZ)]
        vert = lambda x, y, core: {"vert": (x * NY + y) * 2 + core}
        self.sib = vert(self.x, self.y, 1 - self.core)
        self.xp = [vert(a, self.y, self.core) for a in self.xs]
        self.yp = [vert(self.x, a, self.core) for a in self.ys]
        self.zp = [{"frame": a} for a in self.zs]


def send(src, dst, s, r, peer):
    cp = pltpu.make_async_remote_copy(src, dst, s, r, device_id=peer, device_id_type=MESH)
    cp.start()
    return cp


def reduce_steps(pos, d, bufs, sems, sent):
    b0, acc, b1, sub, b2, gat, full = bufs
    whole_y = gat is None
    (s0, r0), (s1, r1), (s2, r2), (s3, r3), (s4, r4), (s5, r5) = sems
    half = d.shape[0] // 2
    q = half // NX
    e = b2.shape[1]
    xs, ys, core = pos.xs, pos.ys, pos.core
    order = (2, 1, 3, 0)
    c0 = [
        send(d.at[pl.ds((1 - core) * half + xs[k] * q, q)], b0.at[i], s0.at[i], r0.at[i], pos.sib)
        for i, k in enumerate(order)
    ]
    sent += c0
    yield
    c1 = {}
    for i, k in enumerate(order):
        c0[i].wait_recv()
        acc[i] = b0[i] + d[pl.ds(core * half + xs[k] * q, q)]
        if k:
            c1[k] = send(acc.at[i], b1.at[k - 1], s1.at[k - 1], r1.at[k - 1], pos.xp[k])
    sent += c1.values()
    yield
    tot = acc[3]
    for k in (1, 3, 2):
        c1[k].wait_recv()
        tot = tot + b1[k - 1]
    sub[0:q] = tot
    if not whole_y and NY * e > q:
        sub[q:] = jnp.zeros((NY * e - q, 8, 128), jnp.float32)
    if whole_y:
        b2[pos.y] = tot
    c2 = {
        k: send(
            sub if whole_y else sub.at[pl.ds(ys[k] * e, e)], b2.at[pos.y if whole_y else k - 1],
            s2.at[k - 1], r2.at[k - 1], pos.yp[k],
        )
        for k in far_first
    }
    sent += c2.values()
    yield
    for k in far_first[::-1]:
        c2[k].wait_recv()
    tot = b2[0]
    for k in range(1, b2.shape[0]):
        tot = tot + b2[k]
    if not whole_y:
        mine = pl.ds(pos.y * e, e)
        tot = tot + sub[mine]
        gat[mine] = tot
        c3 = {
            k: send(gat.at[mine], gat.at[mine], s3.at[k - 1], r3.at[k - 1], pos.yp[k])
            for k in far_first
        }
        sent += c3.values()
        yield
        for k in far_first[::-1]:
            c3[k].wait_recv()
        tot = gat[0:q]
    mine = pl.ds(core * half + pos.x * q, q)
    full[mine] = tot
    c4 = {k: send(full.at[mine], full.at[mine], s4.at[k - 1], r4.at[k - 1], pos.xp[k]) for k in (2, 1, 3)}
    c5 = [send(full.at[mine], full.at[mine], s5.at[0], r5.at[0], pos.sib)]
    sent += c4.values()
    yield
    for i, k in enumerate((1, 3, 2)):
        c4[k].wait_recv()
        blk = pl.ds(core * half + lax.rem(pos.x + NX - k, NX) * q, q)
        c5.append(send(full.at[blk], full.at[blk], s5.at[i + 1], r5.at[i + 1], pos.sib))
    sent += c5
    yield
    for cp in c5:
        cp.wait_recv()
    yield


def kernel(ridge, scale, *refs):
    it = iter(refs)
    take = lambda n: [next(it) for _ in range(n)]
    anim, rest_h, lab_h, prior_h, out, f_out = take(6)
    rows, feats, f_high, f_low, rest, lab, w_ref, dg, dr, g, gb = take(11)
    ez, ey, ex, ec, et = take(5)
    g_bufs, r_bufs = take(6), take(7)
    g_bufs.insert(5, None)
    in_sem, row_sem = take(2)
    pairs = lambda n: [tuple(take(2)) for _ in range(n)]
    g_sems, r_sems = pairs(6), pairs(6)
    (sg, rg), (sa, ra), (sz, rz), (sy, ry), (sx, rx), (sc, rc) = pairs(6)

    n_rows, verts = anim.shape
    bones = prior_h.shape[0]
    joint = 4 * bones
    cv = verts // CHUNKS
    pos = Place()

    small = [
        pltpu.make_async_copy(src, dst, in_sem.at[i])
        for i, (src, dst) in enumerate(((prior_h, w_ref), (rest_h, rest), (lab_h, lab)))
    ]
    for cp in small:
        cp.start()
    for j in range(CHUNKS):
        s = pl.ds(j * cv, cv)
        pltpu.make_async_copy(anim.at[:, s], rows.at[:, s], row_sem.at[j]).start()
    barrier = pltpu.get_barrier_semaphore()
    peers = [pos.sib] + pos.xp[1:] + pos.yp[1:] + pos.zp[1:]
    for p in peers:
        pl.semaphore_signal(barrier, inc=1, device_id=p, device_id_type=MESH)
    for cp in small:
        cp.wait()

    ids = lax.broadcasted_iota(jnp.int32, (bones, cv), 0)

    def gram_chunk(j, gram):
        s = pl.ds(pl.multiple_of(j * cv, cv), cv)
        summed = jnp.where(ids == lab[:, s], 1.0, 0.0) + w_ref[:, s]
        w = summed / jnp.sum(summed, axis=0, keepdims=True)
        w_ref[:, s] = w
        f = jnp.concatenate([w * rest[k : k + 1, s] for k in range(3)] + [w], axis=0)
        feats[:, s] = f
        f_high[:, s], f_low[:, s] = halves(f)
        return gram + hdot(f, f, NT)

    gram = lax.fori_loop(0, CHUNKS, gram_chunk, jnp.zeros((joint, joint), jnp.float32))
    rt = n_rows // 8
    bt = bones // 8
    last = jnp.concatenate([gram[bones : 2 * bones, bones : 2 * bones], gram[3 * bones :, 3 * bones :]], axis=1)
    packed = [gram[:bones, :128], gram[:bones, 128:], gram[bones : 2 * bones, 128:], gram[2 * bones : 3 * bones, 128:], last]
    for i, part in enumerate(packed):
        dg[i * bt : (i + 1) * bt] = part.reshape(bt, 8, 128)
    sent = []
    pl.semaphore_wait(barrier, len(peers))
    gsteps = reduce_steps(pos, dg, g_bufs, g_sems, sent)
    rsteps = reduce_steps(pos, dr, r_bufs, r_sems, sent)
    next(gsteps)

    def rhs_chunk(j, rhs):
        s = pl.ds(pl.multiple_of(j * cv, cv), cv)
        pltpu.make_async_copy(anim.at[:, s], rows.at[:, s], row_sem.at[j]).wait()
        return rhs + hdot(rows[:, s], feats[:, s], NT)

    next(gsteps)
    rhs = lax.fori_loop(0, CHUNKS, rhs_chunk, jnp.zeros((n_rows, joint), jnp.float32))
    for h in range(2):
        dr[h * rt : (h + 1) * rt] = rhs[:, h * 128 : (h + 1) * 128].reshape(rt, 8, 128)
    next(rsteps)
    next(gsteps)
    next(rsteps)
    next(rsteps)
    next(gsteps)
    next(gsteps)
    next(gsteps)
    next(rsteps)

    square = (joint, joint)
    eye = lax.broadcasted_iota(jnp.int32, square, 0) == lax.broadcasted_iota(jnp.int32, square, 1)
    dg, dr = g_bufs[-1], r_bufs[-1]
    p = [dg[i * bt : (i + 1) * bt].reshape(bones, 128) for i in range(5)]
    blocks = {}
    pairs_of = (((0, 0), (0, 1)), ((0, 2), (0, 3)), ((1, 2), (1, 3)), ((2, 2), (2, 3)), ((1, 1), (3, 3)))
    for part, names in zip(p, pairs_of):
        for i, (k, l) in enumerate(names):
            blocks[k, l] = blocks[l, k] = part[:, i * bones : (i + 1) * bones]
    gram = jnp.concatenate(
        [jnp.concatenate([blocks[k, l] for l in range(4)], axis=1) for k in range(4)], axis=0
    )
    gram = gram + jnp.where(eye, ridge, 0.0)
    neg = negative_inverse(gram, 64, 4, lambda i: next(rsteps) if i in (4, 6, 7) else None)
    rhs = jnp.concatenate([dr[h * rt : (h + 1) * rt].reshape(n_rows, 128) for h in range(2)], axis=1)
    tt = -hdot(rhs, neg)
    left = (rhs - hdot(tt, gram)).astype(jnp.bfloat16)
    tt = tt - jnp.dot(left, neg.astype(jnp.bfloat16), preferred_element_type=jnp.float32)
    tt_parts, t_parts = halves(tt), halves(tt.T)

    def fit_chunk(j, squares):
        s = pl.ds(pl.multiple_of(j * cv, cv), cv)
        e = rows[:, s] - dot3(tt_parts, (f_high[:, s], f_low[:, s]))
        pulled = dot3(t_parts, halves(e))
        grad = pulled[3 * bones :]
        for k in range(3):
            grad = grad + pulled[k * bones : (k + 1) * bones] * rest[k : k + 1, s]
        g[:, :, s] = (-2.0 * grad).reshape(NZ, bones // NZ, cv)
        for k in far_first:
            send(g.at[pos.zs[k], :, s], gb.at[k - 1, :, s], sg.at[j, k - 1], rg.at[j, k - 1], pos.zp[k])
        sq = (e * e).reshape(n_rows // 8, 8, cv).sum(axis=0)
        return squares + total([sq[:, i * 128 : (i + 1) * 128] for i in range(cv // 128)])

    et[0] = lax.fori_loop(0, CHUNKS, fit_chunk, jnp.zeros((8, 128), jnp.float32))
    cz = [send(et.at[0], ez.at[pos.z], sz.at[k - 1], rz.at[k - 1], pos.zp[k]) for k in far_first]

    mine = pl.ds(pl.multiple_of(pos.z * (bones // NZ), bones // NZ), bones // NZ)

    def update_chunk(j, carry):
        s = pl.ds(pl.multiple_of(j * cv, cv), cv)
        grad = g[pos.z, :, s]
        for k in far_first[::-1]:
            pltpu.make_async_remote_copy(
                g.at[pos.zs[k], :, s], gb.at[k - 1, :, s], sg.at[j, k - 1], rg.at[j, k - 1],
                device_id=pos.zp[k], device_id_type=MESH,
            ).wait()
            grad = grad + gb[k - 1, :, s]
        out[pos.z, :, s] = jnp.clip(w_ref[mine, s] - step_size * grad, 0.0, 1.0)
        for k in far_first:
            send(out.at[pos.z, :, s], out.at[pos.z, :, s], sa.at[j, k - 1], ra.at[j, k - 1], pos.zp[k])
        return carry

    lax.fori_loop(0, CHUNKS, update_chunk, 0)

    def add_up(copies, buf, at, i):
        buf[at] = et[i]
        for cp in copies:
            cp.wait_recv()
        tot = buf[0]
        for k in range(1, buf.shape[0]):
            tot = tot + buf[k]
        et[i + 1] = tot

    add_up(cz, ez, pos.z, 0)
    cy = [send(et.at[1], ey.at[pos.y], sy.at[k - 1], ry.at[k - 1], pos.yp[k]) for k in far_first]
    add_up(cy, ey, pos.y, 1)
    cx = [send(et.at[2], ex.at[pos.x], sx.at[k - 1], rx.at[k - 1], pos.xp[k]) for k in (2, 1, 3)]
    add_up(cx, ex, pos.x, 2)
    cc = [send(et.at[3], ec.at[0], sc.at[0], rc.at[0], pos.sib)]
    cc[0].wait_recv()
    et[4] = et[3] + ec[0]
    f_out[...] = jnp.sum(et[4], axis=(0, 1), keepdims=True) * scale

    def gather_chunk(j, carry):
        s = pl.ds(pl.multiple_of(j * cv, cv), cv)
        for k in far_first[::-1]:
            pltpu.make_async_remote_copy(
                out.at[pos.z, :, s], out.at[pos.z, :, s], sa.at[j, k - 1], ra.at[j, k - 1],
                device_id=pos.zp[k], device_id_type=MESH,
            ).wait()
        return carry

    lax.fori_loop(0, CHUNKS, gather_chunk, 0)
    for cp in sent + cz + cy + cx + cc:
        cp.wait_send()


def local(animated, rest_positions, labels, weight_prior):
    bones, verts = weight_prior.shape
    n_rows = 3 * animated.shape[0]
    joint = 4 * bones
    verts_total = verts * lax.axis_size("vert")
    frames_total = animated.shape[0] * lax.axis_size("frame")
    rows = animated.transpose(1, 0, 2).reshape(n_rows, verts)

    vmem = lambda *s: pltpu.VMEM(s, jnp.float32)
    tiles = lambda *s: vmem(*s, 8, 128)

    def buffers(n, whole_y):
        q = n // (2 * NX)
        e = -(-q // NY)
        common = [tiles(NX, q), tiles(NX, q), tiles(NX - 1, q)]
        if whole_y:
            return common + [tiles(q), tiles(NY, q), tiles(n)]
        return common + [tiles(NY * e), tiles(NY - 1, e), tiles(NY * e), tiles(n)]

    pair = lambda *s: [pltpu.SemaphoreType.DMA(s)] * 2
    reduce_pairs = pair(4) + pair(3) + pair(7) + pair(7) + pair(3) + pair(4)
    n_gram, n_rhs = 10 * bones * bones // 1024, n_rows * joint // 1024
    scratch = [
        vmem(n_rows, verts), vmem(joint, verts),
        pltpu.VMEM((joint, verts), jnp.bfloat16), pltpu.VMEM((joint, verts), jnp.bfloat16), vmem(3, verts), pltpu.VMEM((1, verts), jnp.int32),
        vmem(bones, verts), tiles(n_gram), tiles(n_rhs), vmem(NZ, bones // NZ, verts),
        vmem(NZ - 1, bones // NZ, verts), tiles(NZ), tiles(NY), tiles(NX), tiles(1), tiles(5),
    ]
    scratch += buffers(n_gram, True) + buffers(n_rhs, False)
    scratch += [pltpu.SemaphoreType.DMA((3,)), pltpu.SemaphoreType.DMA((CHUNKS,))]
    scratch += reduce_pairs + reduce_pairs
    scratch += pair(CHUNKS, NZ - 1) + pair(CHUNKS, NZ - 1) + pair(NZ - 1) + pair(NY - 1) + pair(NX - 1) + pair(1)

    hbm, vm = pl.BlockSpec(memory_space=pltpu.HBM), pl.BlockSpec(memory_space=pltpu.VMEM)
    new_weights, fit_error = pl.pallas_call(
        functools.partial(kernel, ridge_scale * verts_total, 1.0 / (3.0 * frames_total * verts_total)),
        out_shape=(
            jax.ShapeDtypeStruct((NZ, bones // NZ, verts), jnp.float32),
            jax.ShapeDtypeStruct((1, 1), jnp.float32),
        ),
        in_specs=[hbm] * 4,
        out_specs=(vm, vm),
        scratch_shapes=scratch,
        compiler_params=pltpu.CompilerParams(
            collective_id=0, has_side_effects=True, vmem_limit_bytes=56 << 20
        ),
        name="skinning",
    )(rows, rest_positions, labels.reshape(1, verts), weight_prior)
    return new_weights.reshape(bones, verts), fit_error.reshape(())


def solution(mesh):
    placed = (P("frame", None, "vert"), P(None, "vert"), P("vert"), P(None, "vert"))
    return jax.shard_map(
        local, mesh=mesh, in_specs=placed, out_specs=(P(None, "vert"), P()), check_vma=False
    )
```

```python
import functools

import jax
import jax.numpy as jnp
from jax import lax
from jax.experimental import pallas as pl
from jax.experimental.pallas import tpu as pltpu
from jax.sharding import PartitionSpec as P

HI = lax.Precision.HIGHEST
MESH = pl.DeviceIdType.MESH
NT = (((1,), (1,)), ((), ()))
NN = (((1,), (0,)), ((), ()))
TN = (((0,), (0,)), ((), ()))
NX, NY, NZ = 4, 8, 8
CHUNKS = 4
ridge_scale = 0.0001
step_size = 0.005
far_first = (4, 3, 5, 2, 6, 1, 7)


def hdot(a, b, dims=NN):
    return lax.dot_general(a, b, dims, precision=HI, preferred_element_type=jnp.float32)


def halves(a):
    high = a.astype(jnp.bfloat16)
    return high, (a - high.astype(jnp.float32)).astype(jnp.bfloat16)


def dot3(a, b):
    dot = lambda x, y: lax.dot_general(x, y, NN, preferred_element_type=jnp.float32)
    return dot(a[0], b[0]) + (dot(a[0], b[1]) + dot(a[1], b[0]))


def sym(f, n):
    m = [[None] * n for _ in range(n)]
    for i in range(n):
        for j in range(i, n):
            m[i][j] = m[j][i] = f(i, j)
    return m


def total(terms):
    while len(terms) > 1:
        terms = [terms[i] + terms[i + 1] for i in range(0, len(terms) - 1, 2)] + (
            [terms[-1]] if len(terms) % 2 else []
        )
    return terms[0]


def inv_sym(m):
    n = len(m)
    if n == 2:
        r = 1.0 / (m[0][0] * m[1][1] - m[0][1] * m[0][1])
        b = -m[0][1] * r
        return [[m[1][1] * r, b], [b, m[0][0] * r]]
    h = n // 2
    rng = range(h)
    a = inv_sym([row[:h] for row in m[:h]])
    f = [row[h:] for row in m[:h]]
    af = [[total([a[i][l] * f[l][j] for l in rng]) for j in rng] for i in rng]
    s = inv_sym(sym(lambda i, j: m[h + i][h + j] - total([f[l][i] * af[l][j] for l in rng]), h))
    off = [[-total([af[i][l] * s[l][j] for l in rng]) for j in rng] for i in rng]
    top = sym(lambda i, j: a[i][j] - total([off[i][l] * af[j][l] for l in rng]), h)
    return [top[i] + off[i] for i in rng] + [[off[j][i] for j in rng] + s[i] for i in rng]


def sweep(p, b, halfway):
    n = p.shape[0]
    sub = lax.broadcasted_iota(jnp.int32, (n, n), 0)
    lane = lax.broadcasted_iota(jnp.int32, (n, n), 1)
    lane1 = lane[0:1]
    for k in range(0, n, b):
        if k == n // 2:
            halfway()
        c = [jnp.broadcast_to(p[:, k + j : k + j + 1], (n, n)) for j in range(b)]
        m = inv_sym(sym(lambda i, j: c[j][k + i : k + i + 1], b))
        r = [
            jnp.where(lane1 == k + j, -1.0, jnp.where(lane1 // b == k // b, 0.0, p[k + j : k + j + 1]))
            for j in range(b)
        ]
        w = [total([m[i][j] * r[j] for j in range(b)]) for i in range(b)]
        c = [jnp.where(sub == k + j, -1.0, jnp.where(sub // b == k // b, 0.0, c[j])) for j in range(b)]
        keep = jnp.where((sub // b == k // b) | (lane // b == k // b), 0.0, p)
        p = keep - total([c[j] * w[j] for j in range(b)])
    return p


def negative_inverse(a, nb, b, between):
    n = a.shape[0]
    sub = lax.broadcasted_iota(jnp.int32, (n, n), 0) // nb
    lane = lax.broadcasted_iota(jnp.int32, (n, n), 1) // nb
    square = (nb, nb)
    eye = (
        lax.broadcasted_iota(jnp.int32, square, 0) == lax.broadcasted_iota(jnp.int32, square, 1)
    ).astype(jnp.float32)
    for i in range(n // nb):
        s = i * nb
        rows = a[s : s + nb]
        neg = sweep(rows[:, s : s + nb], b, lambda: between(2 * i))
        if i == n // nb - 1:
            between(2 * i + 1)
        w = -hdot(neg, rows)

        def parts(middle, full):
            left = [full[:, :s]] if s else []
            right = [full[:, s + nb :]] if s + nb < n else []
            return jnp.concatenate(left + [middle] + right, axis=1)

        a = jnp.where((sub == i) | (lane == i), 0.0, a) - hdot(parts(-eye, rows), parts(neg, w), TN)
        between(2 * i + 1 + i // (n // nb - 1))
    return a


class Place:
    def __init__(self):
        me = lax.axis_index("vert")
        self.core = lax.rem(me, 2)
        self.y = lax.rem(me // 2, NY)
        self.x = me // (2 * NY)
        self.z = lax.axis_index("frame")
        self.xs = [lax.rem(self.x + k, NX) for k in range(NX)]
        self.ys = [lax.rem(self.y + k, NY) for k in range(NY)]
        self.zs = [lax.rem(self.z + k, NZ) for k in range(NZ)]
        vert = lambda x, y, core: {"vert": (x * NY + y) * 2 + core}
        self.sib = vert(self.x, self.y, 1 - self.core)
        self.xp = [vert(a, self.y, self.core) for a in self.xs]
        self.yp = [vert(self.x, a, self.core) for a in self.ys]
        self.zp = [{"frame": a} for a in self.zs]


def send(src, dst, s, r, peer):
    cp = pltpu.make_async_remote_copy(src, dst, s, r, device_id=peer, device_id_type=MESH)
    cp.start()
    return cp


def reduce_steps(pos, d, bufs, sems, sent):
    b0, acc, b1, sub, b2, gat, full = bufs
    whole_y = gat is None
    (s0, r0), (s1, r1), (s2, r2), (s3, r3), (s4, r4), (s5, r5) = sems
    half = d.shape[0] // 2
    q = half // NX
    e = b2.shape[1]
    xs, ys, core = pos.xs, pos.ys, pos.core
    order = (2, 1, 3, 0)
    c0 = [
        send(d.at[pl.ds((1 - core) * half + xs[k] * q, q)], b0.at[i], s0.at[i], r0.at[i], pos.sib)
        for i, k in enumerate(order)
    ]
    sent += c0
    yield
    c1 = {}
    for i, k in enumerate(order):
        c0[i].wait_recv()
        acc[i] = b0[i] + d[pl.ds(core * half + xs[k] * q, q)]
        if k:
            c1[k] = send(acc.at[i], b1.at[k - 1], s1.at[k - 1], r1.at[k - 1], pos.xp[k])
    sent += c1.values()
    yield
    tot = acc[3]
    for k in (1, 3, 2):
        c1[k].wait_recv()
        tot = tot + b1[k - 1]
    sub[0:q] = tot
    if not whole_y and NY * e > q:
        sub[q:] = jnp.zeros((NY * e - q, 8, 128), jnp.float32)
    if whole_y:
        b2[pos.y] = tot
    c2 = {
        k: send(
            sub if whole_y else sub.at[pl.ds(ys[k] * e, e)], b2.at[pos.y if whole_y else k - 1],
            s2.at[k - 1], r2.at[k - 1], pos.yp[k],
        )
        for k in far_first
    }
    sent += c2.values()
    yield
    for k in far_first[::-1]:
        c2[k].wait_recv()
    tot = b2[0]
    for k in range(1, b2.shape[0]):
        tot = tot + b2[k]
    if not whole_y:
        mine = pl.ds(pos.y * e, e)
        tot = tot + sub[mine]
        gat[mine] = tot
        c3 = {
            k: send(gat.at[mine], gat.at[mine], s3.at[k - 1], r3.at[k - 1], pos.yp[k])
            for k in far_first
        }
        sent += c3.values()
        yield
        for k in far_first[::-1]:
            c3[k].wait_recv()
        tot = gat[0:q]
    mine = pl.ds(core * half + pos.x * q, q)
    full[mine] = tot
    c4 = {k: send(full.at[mine], full.at[mine], s4.at[k - 1], r4.at[k - 1], pos.xp[k]) for k in (2, 1, 3)}
    c5 = [send(full.at[mine], full.at[mine], s5.at[0], r5.at[0], pos.sib)]
    sent += c4.values()
    yield
    for i, k in enumerate((1, 3, 2)):
        c4[k].wait_recv()
        blk = pl.ds(core * half + lax.rem(pos.x + NX - k, NX) * q, q)
        c5.append(send(full.at[blk], full.at[blk], s5.at[i + 1], r5.at[i + 1], pos.sib))
    sent += c5
    yield
    for cp in c5:
        cp.wait_recv()
    yield


def kernel(ridge, scale, *refs):
    it = iter(refs)
    take = lambda n: [next(it) for _ in range(n)]
    anim, rest_h, lab_h, prior_h, out, f_out = take(6)
    rows, feats, rest, lab, w_ref, dg, dr, g, gb = take(9)
    ez, ey, ex, ec, et = take(5)
    g_bufs, r_bufs = take(6), take(7)
    g_bufs.insert(5, None)
    in_sem, row_sem = take(2)
    pairs = lambda n: [tuple(take(2)) for _ in range(n)]
    g_sems, r_sems = pairs(6), pairs(6)
    (sg, rg), (sa, ra), (sz, rz), (sy, ry), (sx, rx), (sc, rc) = pairs(6)

    n_rows, verts = anim.shape
    bones = prior_h.shape[0]
    joint = 4 * bones
    cv = verts // CHUNKS
    pos = Place()

    small = [
        pltpu.make_async_copy(src, dst, in_sem.at[i])
        for i, (src, dst) in enumerate(((prior_h, w_ref), (rest_h, rest), (lab_h, lab)))
    ]
    for cp in small:
        cp.start()
    for j in range(CHUNKS):
        s = pl.ds(j * cv, cv)
        pltpu.make_async_copy(anim.at[:, s], rows.at[:, s], row_sem.at[j]).start()
    barrier = pltpu.get_barrier_semaphore()
    peers = [pos.sib] + pos.xp[1:] + pos.yp[1:] + pos.zp[1:]
    for p in peers:
        pl.semaphore_signal(barrier, inc=1, device_id=p, device_id_type=MESH)
    for cp in small:
        cp.wait()

    ids = lax.broadcasted_iota(jnp.int32, (bones, cv), 0)

    def gram_chunk(j, gram):
        s = pl.ds(pl.multiple_of(j * cv, cv), cv)
        summed = jnp.where(ids == lab[:, s], 1.0, 0.0) + w_ref[:, s]
        w = summed / jnp.sum(summed, axis=0, keepdims=True)
        w_ref[:, s] = w
        f = jnp.concatenate([w * rest[k : k + 1, s] for k in range(3)] + [w], axis=0)
        feats[:, s] = f
        return gram + hdot(f, f, NT)

    gram = lax.fori_loop(0, CHUNKS, gram_chunk, jnp.zeros((joint, joint), jnp.float32))
    rt = n_rows // 8
    bt = bones // 8
    last = jnp.concatenate([gram[bones : 2 * bones, bones : 2 * bones], gram[3 * bones :, 3 * bones :]], axis=1)
    packed = [gram[:bones, :128], gram[:bones, 128:], gram[bones : 2 * bones, 128:], gram[2 * bones : 3 * bones, 128:], last]
    for i, part in enumerate(packed):
        dg[i * bt : (i + 1) * bt] = part.reshape(bt, 8, 128)
    sent = []
    pl.semaphore_wait(barrier, len(peers))
    gsteps = reduce_steps(pos, dg, g_bufs, g_sems, sent)
    rsteps = reduce_steps(pos, dr, r_bufs, r_sems, sent)
    next(gsteps)

    def rhs_chunk(j, rhs):
        s = pl.ds(pl.multiple_of(j * cv, cv), cv)
        pltpu.make_async_copy(anim.at[:, s], rows.at[:, s], row_sem.at[j]).wait()
        return rhs + hdot(rows[:, s], feats[:, s], NT)

    next(gsteps)
    rhs = lax.fori_loop(0, CHUNKS, rhs_chunk, jnp.zeros((n_rows, joint), jnp.float32))
    for h in range(2):
        dr[h * rt : (h + 1) * rt] = rhs[:, h * 128 : (h + 1) * 128].reshape(rt, 8, 128)
    next(rsteps)
    next(gsteps)
    next(rsteps)
    next(rsteps)
    next(gsteps)
    next(gsteps)
    next(gsteps)
    next(rsteps)

    square = (joint, joint)
    eye = lax.broadcasted_iota(jnp.int32, square, 0) == lax.broadcasted_iota(jnp.int32, square, 1)
    dg, dr = g_bufs[-1], r_bufs[-1]
    p = [dg[i * bt : (i + 1) * bt].reshape(bones, 128) for i in range(5)]
    blocks = {}
    pairs_of = (((0, 0), (0, 1)), ((0, 2), (0, 3)), ((1, 2), (1, 3)), ((2, 2), (2, 3)), ((1, 1), (3, 3)))
    for part, names in zip(p, pairs_of):
        for i, (k, l) in enumerate(names):
            blocks[k, l] = blocks[l, k] = part[:, i * bones : (i + 1) * bones]
    gram = jnp.concatenate(
        [jnp.concatenate([blocks[k, l] for l in range(4)], axis=1) for k in range(4)], axis=0
    )
    gram = gram + jnp.where(eye, ridge, 0.0)
    neg = negative_inverse(gram, 64, 4, lambda i: next(rsteps) if i in (3, 7, 8) else None)
    rhs = jnp.concatenate([dr[h * rt : (h + 1) * rt].reshape(n_rows, 128) for h in range(2)], axis=1)
    neg_parts = halves(neg)
    tt = -dot3(halves(rhs), neg_parts)
    tt = tt - dot3(halves(rhs - hdot(tt, gram)), neg_parts)
    t_parts = halves(tt.T)

    def fit_chunk(j, squares):
        s = pl.ds(pl.multiple_of(j * cv, cv), cv)
        e = rows[:, s] - hdot(tt, feats[:, s])
        pulled = dot3(t_parts, halves(e))
        grad = pulled[3 * bones :]
        for k in range(3):
            grad = grad + pulled[k * bones : (k + 1) * bones] * rest[k : k + 1, s]
        g[:, :, s] = (-2.0 * grad).reshape(NZ, bones // NZ, cv)
        for k in far_first:
            send(g.at[pos.zs[k], :, s], gb.at[k - 1, :, s], sg.at[j, k - 1], rg.at[j, k - 1], pos.zp[k])
        sq = (e * e).reshape(n_rows // 8, 8, cv).sum(axis=0)
        return squares + total([sq[:, i * 128 : (i + 1) * 128] for i in range(cv // 128)])

    et[0] = lax.fori_loop(0, CHUNKS, fit_chunk, jnp.zeros((8, 128), jnp.float32))
    cz = [send(et.at[0], ez.at[pos.z], sz.at[k - 1], rz.at[k - 1], pos.zp[k]) for k in far_first]

    mine = pl.ds(pl.multiple_of(pos.z * (bones // NZ), bones // NZ), bones // NZ)

    def update_chunk(j, carry):
        s = pl.ds(pl.multiple_of(j * cv, cv), cv)
        grad = g[pos.z, :, s]
        for k in far_first[::-1]:
            pltpu.make_async_remote_copy(
                g.at[pos.zs[k], :, s], gb.at[k - 1, :, s], sg.at[j, k - 1], rg.at[j, k - 1],
                device_id=pos.zp[k], device_id_type=MESH,
            ).wait()
            grad = grad + gb[k - 1, :, s]
        out[pos.z, :, s] = jnp.clip(w_ref[mine, s] - step_size * grad, 0.0, 1.0)
        for k in far_first:
            send(out.at[pos.z, :, s], out.at[pos.z, :, s], sa.at[j, k - 1], ra.at[j, k - 1], pos.zp[k])
        return carry

    lax.fori_loop(0, CHUNKS, update_chunk, 0)

    def add_up(copies, buf, at, i):
        buf[at] = et[i]
        for cp in copies:
            cp.wait_recv()
        tot = buf[0]
        for k in range(1, buf.shape[0]):
            tot = tot + buf[k]
        et[i + 1] = tot

    add_up(cz, ez, pos.z, 0)
    cy = [send(et.at[1], ey.at[pos.y], sy.at[k - 1], ry.at[k - 1], pos.yp[k]) for k in far_first]
    add_up(cy, ey, pos.y, 1)
    cx = [send(et.at[2], ex.at[pos.x], sx.at[k - 1], rx.at[k - 1], pos.xp[k]) for k in (2, 1, 3)]
    add_up(cx, ex, pos.x, 2)
    cc = [send(et.at[3], ec.at[0], sc.at[0], rc.at[0], pos.sib)]
    cc[0].wait_recv()
    et[4] = et[3] + ec[0]
    f_out[...] = jnp.sum(et[4], axis=(0, 1), keepdims=True) * scale

    def gather_chunk(j, carry):
        s = pl.ds(pl.multiple_of(j * cv, cv), cv)
        for k in far_first[::-1]:
            pltpu.make_async_remote_copy(
                out.at[pos.z, :, s], out.at[pos.z, :, s], sa.at[j, k - 1], ra.at[j, k - 1],
                device_id=pos.zp[k], device_id_type=MESH,
            ).wait()
        return carry

    lax.fori_loop(0, CHUNKS, gather_chunk, 0)
    for cp in sent + cz + cy + cx + cc:
        cp.wait_send()


def local(animated, rest_positions, labels, weight_prior):
    bones, verts = weight_prior.shape
    n_rows = 3 * animated.shape[0]
    joint = 4 * bones
    verts_total = verts * lax.axis_size("vert")
    frames_total = animated.shape[0] * lax.axis_size("frame")
    rows = animated.transpose(1, 0, 2).reshape(n_rows, verts)

    vmem = lambda *s: pltpu.VMEM(s, jnp.float32)
    tiles = lambda *s: vmem(*s, 8, 128)

    def buffers(n, whole_y):
        q = n // (2 * NX)
        e = -(-q // NY)
        common = [tiles(NX, q), tiles(NX, q), tiles(NX - 1, q)]
        if whole_y:
            return common + [tiles(q), tiles(NY, q), tiles(n)]
        return common + [tiles(NY * e), tiles(NY - 1, e), tiles(NY * e), tiles(n)]

    pair = lambda *s: [pltpu.SemaphoreType.DMA(s)] * 2
    reduce_pairs = pair(4) + pair(3) + pair(7) + pair(7) + pair(3) + pair(4)
    n_gram, n_rhs = 10 * bones * bones // 1024, n_rows * joint // 1024
    scratch = [
        vmem(n_rows, verts), vmem(joint, verts),
        vmem(3, verts), pltpu.VMEM((1, verts), jnp.int32),
        vmem(bones, verts), tiles(n_gram), tiles(n_rhs), vmem(NZ, bones // NZ, verts),
        vmem(NZ - 1, bones // NZ, verts), tiles(NZ), tiles(NY), tiles(NX), tiles(1), tiles(5),
    ]
    scratch += buffers(n_gram, True) + buffers(n_rhs, False)
    scratch += [pltpu.SemaphoreType.DMA((3,)), pltpu.SemaphoreType.DMA((CHUNKS,))]
    scratch += reduce_pairs + reduce_pairs
    scratch += pair(CHUNKS, NZ - 1) + pair(CHUNKS, NZ - 1) + pair(NZ - 1) + pair(NY - 1) + pair(NX - 1) + pair(1)

    hbm, vm = pl.BlockSpec(memory_space=pltpu.HBM), pl.BlockSpec(memory_space=pltpu.VMEM)
    new_weights, fit_error = pl.pallas_call(
        functools.partial(kernel, ridge_scale * verts_total, 1.0 / (3.0 * frames_total * verts_total)),
        out_shape=(
            jax.ShapeDtypeStruct((NZ, bones // NZ, verts), jnp.float32),
            jax.ShapeDtypeStruct((1, 1), jnp.float32),
        ),
        in_specs=[hbm] * 4,
        out_specs=(vm, vm),
        scratch_shapes=scratch,
        compiler_params=pltpu.CompilerParams(
            collective_id=0, has_side_effects=True, vmem_limit_bytes=28 << 20
        ),
        name="skinning",
    )(*[pltpu.with_memory_space_constraint(a, pltpu.HBM) for a in (rows, rest_positions, labels.reshape(1, verts), weight_prior)])
    return new_weights.reshape(bones, verts), fit_error.reshape(())


def solution(mesh):
    placed = (P("frame", None, "vert"), P(None, "vert"), P("vert"), P(None, "vert"))
    return jax.shard_map(
        local, mesh=mesh, in_specs=placed, out_specs=(P(None, "vert"), P()), check_vma=False
    )
```

```python
import functools

import jax
import jax.numpy as jnp
from jax import lax
from jax.experimental import pallas as pl
from jax.experimental.pallas import tpu as pltpu
from jax.sharding import PartitionSpec as P

HI = lax.Precision.HIGHEST
MESH = pl.DeviceIdType.MESH
NT = (((1,), (1,)), ((), ()))
NN = (((1,), (0,)), ((), ()))
TN = (((0,), (0,)), ((), ()))
NX, NY, NZ = 4, 8, 8
CHUNKS = 4
ridge_scale = 0.0001
step_size = 0.005
far_first = (4, 3, 5, 2, 6, 1, 7)


def hdot(a, b, dims=NN):
    return lax.dot_general(a, b, dims, precision=HI, preferred_element_type=jnp.float32)


def halves(a):
    high = a.astype(jnp.bfloat16)
    return high, (a - high.astype(jnp.float32)).astype(jnp.bfloat16)


def dot3(a, b):
    dot = lambda x, y: lax.dot_general(x, y, NN, preferred_element_type=jnp.float32)
    return dot(a[0], b[0]) + (dot(a[0], b[1]) + dot(a[1], b[0]))


def sym(f, n):
    m = [[None] * n for _ in range(n)]
    for i in range(n):
        for j in range(i, n):
            m[i][j] = m[j][i] = f(i, j)
    return m


def total(terms):
    while len(terms) > 1:
        terms = [terms[i] + terms[i + 1] for i in range(0, len(terms) - 1, 2)] + (
            [terms[-1]] if len(terms) % 2 else []
        )
    return terms[0]


def inv_sym(m):
    n = len(m)
    if n == 2:
        r = 1.0 / (m[0][0] * m[1][1] - m[0][1] * m[0][1])
        b = -m[0][1] * r
        return [[m[1][1] * r, b], [b, m[0][0] * r]]
    h = n // 2
    rng = range(h)
    a = inv_sym([row[:h] for row in m[:h]])
    f = [row[h:] for row in m[:h]]
    af = [[total([a[i][l] * f[l][j] for l in rng]) for j in rng] for i in rng]
    s = inv_sym(sym(lambda i, j: m[h + i][h + j] - total([f[l][i] * af[l][j] for l in rng]), h))
    off = [[-total([af[i][l] * s[l][j] for l in rng]) for j in rng] for i in rng]
    top = sym(lambda i, j: a[i][j] - total([off[i][l] * af[j][l] for l in rng]), h)
    return [top[i] + off[i] for i in rng] + [[off[j][i] for j in rng] + s[i] for i in rng]


def sweep(p, b, late):
    n = p.shape[0]
    sub = lax.broadcasted_iota(jnp.int32, (n, n), 0)
    lane = lax.broadcasted_iota(jnp.int32, (n, n), 1)
    lane1 = lane[0:1]
    for k in range(0, n, b):
        if k == 3 * n // 4:
            late()
        c = [jnp.broadcast_to(p[:, k + j : k + j + 1], (n, n)) for j in range(b)]
        m = inv_sym(sym(lambda i, j: c[j][k + i : k + i + 1], b))
        r = [
            jnp.where(lane1 == k + j, -1.0, jnp.where(lane1 // b == k // b, 0.0, p[k + j : k + j + 1]))
            for j in range(b)
        ]
        w = [total([m[i][j] * r[j] for j in range(b)]) for i in range(b)]
        c = [jnp.where(sub == k + j, -1.0, jnp.where(sub // b == k // b, 0.0, c[j])) for j in range(b)]
        keep = jnp.where((sub // b == k // b) | (lane // b == k // b), 0.0, p)
        p = keep - total([c[j] * w[j] for j in range(b)])
    return p


def negative_inverse(a, nb, b, between):
    n = a.shape[0]
    sub = lax.broadcasted_iota(jnp.int32, (n, n), 0) // nb
    lane = lax.broadcasted_iota(jnp.int32, (n, n), 1) // nb
    square = (nb, nb)
    eye = (
        lax.broadcasted_iota(jnp.int32, square, 0) == lax.broadcasted_iota(jnp.int32, square, 1)
    ).astype(jnp.float32)
    for i in range(n // nb):
        s = i * nb
        rows = a[s : s + nb]
        neg = sweep(rows[:, s : s + nb], b, lambda: between(2 * i))
        if i == n // nb - 1:
            between(2 * i + 1)
        w = -hdot(neg, rows)

        def parts(middle, full):
            left = [full[:, :s]] if s else []
            right = [full[:, s + nb :]] if s + nb < n else []
            return jnp.concatenate(left + [middle] + right, axis=1)

        a = jnp.where((sub == i) | (lane == i), 0.0, a) - hdot(parts(-eye, rows), parts(neg, w), TN)
        between(2 * i + 1 + i // (n // nb - 1))
    return a


class Place:
    def __init__(self):
        me = lax.axis_index("vert")
        self.core = lax.rem(me, 2)
        self.y = lax.rem(me // 2, NY)
        self.x = me // (2 * NY)
        self.z = lax.axis_index("frame")
        self.xs = [lax.rem(self.x + k, NX) for k in range(NX)]
        self.ys = [lax.rem(self.y + k, NY) for k in range(NY)]
        self.zs = [lax.rem(self.z + k, NZ) for k in range(NZ)]
        vert = lambda x, y, core: {"vert": (x * NY + y) * 2 + core}
        self.sib = vert(self.x, self.y, 1 - self.core)
        self.xp = [vert(a, self.y, self.core) for a in self.xs]
        self.yp = [vert(self.x, a, self.core) for a in self.ys]
        self.zp = [{"frame": a} for a in self.zs]


def send(src, dst, s, r, peer):
    cp = pltpu.make_async_remote_copy(src, dst, s, r, device_id=peer, device_id_type=MESH)
    cp.start()
    return cp


def reduce_steps(pos, d, bufs, sems, sent):
    b0, acc, b1, sub, b2, gat, full = bufs
    whole_y = gat is None
    (s0, r0), (s1, r1), (s2, r2), (s3, r3), (s4, r4), (s5, r5) = sems
    half = d.shape[0] // 2
    q = half // NX
    e = b2.shape[1]
    xs, ys, core = pos.xs, pos.ys, pos.core
    order = (2, 1, 3, 0)
    c0 = [
        send(d.at[pl.ds((1 - core) * half + xs[k] * q, q)], b0.at[i], s0.at[i], r0.at[i], pos.sib)
        for i, k in enumerate(order)
    ]
    sent += c0
    yield
    c1 = {}
    for i, k in enumerate(order):
        c0[i].wait_recv()
        acc[i] = b0[i] + d[pl.ds(core * half + xs[k] * q, q)]
        if k:
            c1[k] = send(acc.at[i], b1.at[k - 1], s1.at[k - 1], r1.at[k - 1], pos.xp[k])
    sent += c1.values()
    yield
    tot = acc[3]
    for k in (1, 3, 2):
        c1[k].wait_recv()
        tot = tot + b1[k - 1]
    sub[0:q] = tot
    if not whole_y and NY * e > q:
        sub[q:] = jnp.zeros((NY * e - q, 8, 128), jnp.float32)
    if whole_y:
        b2[pos.y] = tot
    c2 = {
        k: send(
            sub if whole_y else sub.at[pl.ds(ys[k] * e, e)], b2.at[pos.y if whole_y else k - 1],
            s2.at[k - 1], r2.at[k - 1], pos.yp[k],
        )
        for k in far_first
    }
    sent += c2.values()
    yield
    for k in far_first[::-1]:
        c2[k].wait_recv()
    tot = b2[0]
    for k in range(1, b2.shape[0]):
        tot = tot + b2[k]
    if not whole_y:
        mine = pl.ds(pos.y * e, e)
        tot = tot + sub[mine]
        gat[mine] = tot
        c3 = {
            k: send(gat.at[mine], gat.at[mine], s3.at[k - 1], r3.at[k - 1], pos.yp[k])
            for k in far_first
        }
        sent += c3.values()
        yield
        for k in far_first[::-1]:
            c3[k].wait_recv()
        tot = gat[0:q]
    mine = pl.ds(core * half + pos.x * q, q)
    full[mine] = tot
    c4 = {k: send(full.at[mine], full.at[mine], s4.at[k - 1], r4.at[k - 1], pos.xp[k]) for k in (2, 1, 3)}
    c5 = [send(full.at[mine], full.at[mine], s5.at[0], r5.at[0], pos.sib)]
    sent += c4.values()
    yield
    for i, k in enumerate((1, 3, 2)):
        c4[k].wait_recv()
        blk = pl.ds(core * half + lax.rem(pos.x + NX - k, NX) * q, q)
        c5.append(send(full.at[blk], full.at[blk], s5.at[i + 1], r5.at[i + 1], pos.sib))
    sent += c5
    yield
    for cp in c5:
        cp.wait_recv()
    yield


def kernel(ridge, scale, *refs):
    it = iter(refs)
    take = lambda n: [next(it) for _ in range(n)]
    anim, rest_h, lab_h, prior_h, out, f_out = take(6)
    rows, feats, rest, lab, w_ref, dg, dr, g, gb = take(9)
    ez, ey, ex, ec, et = take(5)
    g_bufs, r_bufs = take(6), take(7)
    g_bufs.insert(5, None)
    in_sem, row_sem = take(2)
    pairs = lambda n: [tuple(take(2)) for _ in range(n)]
    g_sems, r_sems = pairs(6), pairs(6)
    (sg, rg), (sa, ra), (sz, rz), (sy, ry), (sx, rx), (sc, rc) = pairs(6)

    n_rows, verts = anim.shape
    bones = prior_h.shape[0]
    joint = 4 * bones
    cv = verts // CHUNKS
    pos = Place()

    barrier = pltpu.get_barrier_semaphore()
    peers = [pos.sib] + pos.xp[1:] + pos.yp[1:] + pos.zp[1:]
    for p in peers:
        pl.semaphore_signal(barrier, inc=1, device_id=p, device_id_type=MESH)
    small = [
        pltpu.make_async_copy(src, dst, in_sem.at[i])
        for i, (src, dst) in enumerate(((prior_h, w_ref), (rest_h, rest), (lab_h, lab)))
    ]
    for cp in small:
        cp.start()
    for j in range(CHUNKS):
        s = pl.ds(j * cv, cv)
        pltpu.make_async_copy(anim.at[:, s], rows.at[:, s], row_sem.at[j]).start()
    for cp in small:
        cp.wait()

    ids = lax.broadcasted_iota(jnp.int32, (bones, cv), 0)

    def gram_chunk(j, gram):
        s = pl.ds(pl.multiple_of(j * cv, cv), cv)
        summed = jnp.where(ids == lab[:, s], 1.0, 0.0) + w_ref[:, s]
        w = summed / jnp.sum(summed, axis=0, keepdims=True)
        w_ref[:, s] = w
        f = jnp.concatenate([w * rest[k : k + 1, s] for k in range(3)] + [w], axis=0)
        feats[:, s] = f
        return gram + hdot(f, f, NT)

    gram = lax.fori_loop(0, CHUNKS, gram_chunk, jnp.zeros((joint, joint), jnp.float32))
    rt = n_rows // 8
    bt = bones // 8
    last = jnp.concatenate([gram[bones : 2 * bones, bones : 2 * bones], gram[3 * bones :, 3 * bones :]], axis=1)
    packed = [gram[:bones, :128], gram[:bones, 128:], gram[bones : 2 * bones, 128:], gram[2 * bones : 3 * bones, 128:], last]
    for i, part in enumerate(packed):
        dg[i * bt : (i + 1) * bt] = part.reshape(bt, 8, 128)
    sent = []
    pl.semaphore_wait(barrier, len(peers))
    gsteps = reduce_steps(pos, dg, g_bufs, g_sems, sent)
    rsteps = reduce_steps(pos, dr, r_bufs, r_sems, sent)
    next(gsteps)

    def rhs_chunk(j, rhs):
        s = pl.ds(pl.multiple_of(j * cv, cv), cv)
        pltpu.make_async_copy(anim.at[:, s], rows.at[:, s], row_sem.at[j]).wait()
        return rhs + hdot(rows[:, s], feats[:, s], NT)

    rhs = lax.fori_loop(0, 1, rhs_chunk, jnp.zeros((n_rows, joint), jnp.float32))
    next(gsteps)
    rhs = lax.fori_loop(1, CHUNKS, rhs_chunk, rhs)
    for h in range(2):
        dr[h * rt : (h + 1) * rt] = rhs[:, h * 128 : (h + 1) * 128].reshape(rt, 8, 128)
    next(rsteps)
    next(rsteps)
    next(gsteps)
    next(rsteps)
    next(gsteps)
    next(rsteps)
    next(gsteps)
    next(gsteps)

    square = (joint, joint)
    eye = lax.broadcasted_iota(jnp.int32, square, 0) == lax.broadcasted_iota(jnp.int32, square, 1)
    dg, dr = g_bufs[-1], r_bufs[-1]
    p = [dg[i * bt : (i + 1) * bt].reshape(bones, 128) for i in range(5)]
    blocks = {}
    pairs_of = (((0, 0), (0, 1)), ((0, 2), (0, 3)), ((1, 2), (1, 3)), ((2, 2), (2, 3)), ((1, 1), (3, 3)))
    for part, names in zip(p, pairs_of):
        for i, (k, l) in enumerate(names):
            blocks[k, l] = blocks[l, k] = part[:, i * bones : (i + 1) * bones]
    gram = jnp.concatenate(
        [jnp.concatenate([blocks[k, l] for l in range(4)], axis=1) for k in range(4)], axis=0
    )
    gram = gram + jnp.where(eye, ridge, 0.0)
    neg = negative_inverse(gram, 64, 4, lambda i: next(rsteps) if i in (2, 7, 8) else None)
    rhs = jnp.concatenate([dr[h * rt : (h + 1) * rt].reshape(n_rows, 128) for h in range(2)], axis=1)
    neg_parts = halves(neg)
    tt = -dot3(halves(rhs), neg_parts)
    tt = tt - dot3(halves(rhs - hdot(tt, gram)), neg_parts)
    t_parts = halves(tt.T)

    def fit_chunk(j, squares):
        s = pl.ds(pl.multiple_of(j * cv, cv), cv)
        e = rows[:, s] - hdot(tt, feats[:, s])
        pulled = dot3(t_parts, halves(e))
        grad = pulled[3 * bones :]
        for k in range(3):
            grad = grad + pulled[k * bones : (k + 1) * bones] * rest[k : k + 1, s]
        g[:, :, s] = (-2.0 * grad).reshape(NZ, bones // NZ, cv)
        for k in far_first:
            send(g.at[pos.zs[k], :, s], gb.at[k - 1, :, s], sg.at[j, k - 1], rg.at[j, k - 1], pos.zp[k])
        sq = (e * e).reshape(n_rows // 8, 8, cv).sum(axis=0)
        return squares + total([sq[:, i * 128 : (i + 1) * 128] for i in range(cv // 128)])

    et[0] = lax.fori_loop(0, CHUNKS, fit_chunk, jnp.zeros((8, 128), jnp.float32))
    cz = [send(et.at[0], ez.at[pos.z], sz.at[k - 1], rz.at[k - 1], pos.zp[k]) for k in far_first]

    mine = pl.ds(pl.multiple_of(pos.z * (bones // NZ), bones // NZ), bones // NZ)

    def update_chunk(j, carry):
        s = pl.ds(pl.multiple_of(j * cv, cv), cv)
        grad = g[pos.z, :, s]
        for k in far_first[::-1]:
            pltpu.make_async_remote_copy(
                g.at[pos.zs[k], :, s], gb.at[k - 1, :, s], sg.at[j, k - 1], rg.at[j, k - 1],
                device_id=pos.zp[k], device_id_type=MESH,
            ).wait()
            grad = grad + gb[k - 1, :, s]
        out[pos.z, :, s] = jnp.clip(w_ref[mine, s] - step_size * grad, 0.0, 1.0)
        for k in far_first:
            send(out.at[pos.z, :, s], out.at[pos.z, :, s], sa.at[j, k - 1], ra.at[j, k - 1], pos.zp[k])
        return carry

    lax.fori_loop(0, CHUNKS, update_chunk, 0)

    def add_up(copies, buf, at, i):
        buf[at] = et[i]
        for cp in copies:
            cp.wait_recv()
        tot = buf[0]
        for k in range(1, buf.shape[0]):
            tot = tot + buf[k]
        et[i + 1] = tot

    add_up(cz, ez, pos.z, 0)
    cy = [send(et.at[1], ey.at[pos.y], sy.at[k - 1], ry.at[k - 1], pos.yp[k]) for k in far_first]
    add_up(cy, ey, pos.y, 1)
    cx = [send(et.at[2], ex.at[pos.x], sx.at[k - 1], rx.at[k - 1], pos.xp[k]) for k in (2, 1, 3)]
    add_up(cx, ex, pos.x, 2)
    cc = [send(et.at[3], ec.at[0], sc.at[0], rc.at[0], pos.sib)]
    cc[0].wait_recv()
    et[4] = et[3] + ec[0]
    f_out[...] = jnp.sum(et[4], axis=(0, 1), keepdims=True) * scale

    def gather_chunk(j, carry):
        s = pl.ds(pl.multiple_of(j * cv, cv), cv)
        for k in far_first[::-1]:
            pltpu.make_async_remote_copy(
                out.at[pos.z, :, s], out.at[pos.z, :, s], sa.at[j, k - 1], ra.at[j, k - 1],
                device_id=pos.zp[k], device_id_type=MESH,
            ).wait()
        return carry

    lax.fori_loop(0, CHUNKS, gather_chunk, 0)
    for cp in sent + cz + cy + cx + cc:
        cp.wait_send()


def local(animated, rest_positions, labels, weight_prior):
    bones, verts = weight_prior.shape
    n_rows = 3 * animated.shape[0]
    joint = 4 * bones
    verts_total = verts * lax.axis_size("vert")
    frames_total = animated.shape[0] * lax.axis_size("frame")
    rows = animated.transpose(1, 0, 2).reshape(n_rows, verts)

    vmem = lambda *s: pltpu.VMEM(s, jnp.float32)
    tiles = lambda *s: vmem(*s, 8, 128)

    def buffers(n, whole_y):
        q = n // (2 * NX)
        e = -(-q // NY)
        common = [tiles(NX, q), tiles(NX, q), tiles(NX - 1, q)]
        if whole_y:
            return common + [tiles(q), tiles(NY, q), tiles(n)]
        return common + [tiles(NY * e), tiles(NY - 1, e), tiles(NY * e), tiles(n)]

    pair = lambda *s: [pltpu.SemaphoreType.DMA(s)] * 2
    reduce_pairs = pair(4) + pair(3) + pair(7) + pair(7) + pair(3) + pair(4)
    n_gram, n_rhs = 10 * bones * bones // 1024, n_rows * joint // 1024
    scratch = [
        vmem(n_rows, verts), vmem(joint, verts),
        vmem(3, verts), pltpu.VMEM((1, verts), jnp.int32),
        vmem(bones, verts), tiles(n_gram), tiles(n_rhs), vmem(NZ, bones // NZ, verts),
        vmem(NZ - 1, bones // NZ, verts), tiles(NZ), tiles(NY), tiles(NX), tiles(1), tiles(5),
    ]
    scratch += buffers(n_gram, True) + buffers(n_rhs, False)
    scratch += [pltpu.SemaphoreType.DMA((3,)), pltpu.SemaphoreType.DMA((CHUNKS,))]
    scratch += reduce_pairs + reduce_pairs
    scratch += pair(CHUNKS, NZ - 1) + pair(CHUNKS, NZ - 1) + pair(NZ - 1) + pair(NY - 1) + pair(NX - 1) + pair(1)

    hbm, vm = pl.BlockSpec(memory_space=pltpu.HBM), pl.BlockSpec(memory_space=pltpu.VMEM)
    new_weights, fit_error = pl.pallas_call(
        functools.partial(kernel, ridge_scale * verts_total, 1.0 / (3.0 * frames_total * verts_total)),
        out_shape=(
            jax.ShapeDtypeStruct((NZ, bones // NZ, verts), jnp.float32),
            jax.ShapeDtypeStruct((1, 1), jnp.float32),
        ),
        in_specs=[hbm] * 4,
        out_specs=(vm, vm),
        scratch_shapes=scratch,
        compiler_params=pltpu.CompilerParams(
            collective_id=0, has_side_effects=True, vmem_limit_bytes=28 << 20
        ),
        name="skinning",
    )(*[pltpu.with_memory_space_constraint(a, pltpu.HBM) for a in (rows, rest_positions, labels.reshape(1, verts), weight_prior)])
    return new_weights.reshape(bones, verts), fit_error.reshape(())


def solution(mesh):
    placed = (P("frame", None, "vert"), P(None, "vert"), P("vert"), P(None, "vert"))
    return jax.shard_map(
        local, mesh=mesh, in_specs=placed, out_specs=(P(None, "vert"), P()), check_vma=False
    )
```

```python
import functools

import jax
import jax.numpy as jnp
from jax import lax
from jax.experimental import pallas as pl
from jax.experimental.pallas import tpu as pltpu
from jax.sharding import PartitionSpec as P

HI = lax.Precision.HIGHEST
MESH = pl.DeviceIdType.MESH
NT = (((1,), (1,)), ((), ()))
NN = (((1,), (0,)), ((), ()))
TN = (((0,), (0,)), ((), ()))
NX, NY, NZ = 4, 8, 8
CHUNKS = 4
ridge_scale = 0.0001
step_size = 0.005
far_first = (4, 3, 5, 2, 6, 1, 7)


def hdot(a, b, dims=NN):
    return lax.dot_general(a, b, dims, precision=HI, preferred_element_type=jnp.float32)


def halves(a):
    high = a.astype(jnp.bfloat16)
    return high, (a - high.astype(jnp.float32)).astype(jnp.bfloat16)


def dot3(a, b):
    dot = lambda x, y: lax.dot_general(x, y, NN, preferred_element_type=jnp.float32)
    return dot(a[0], b[0]) + (dot(a[0], b[1]) + dot(a[1], b[0]))


def sym(f, n):
    m = [[None] * n for _ in range(n)]
    for i in range(n):
        for j in range(i, n):
            m[i][j] = m[j][i] = f(i, j)
    return m


def total(terms):
    while len(terms) > 1:
        terms = [terms[i] + terms[i + 1] for i in range(0, len(terms) - 1, 2)] + (
            [terms[-1]] if len(terms) % 2 else []
        )
    return terms[0]


def inv_sym(m):
    n = len(m)
    if n == 2:
        r = 1.0 / (m[0][0] * m[1][1] - m[0][1] * m[0][1])
        b = -m[0][1] * r
        return [[m[1][1] * r, b], [b, m[0][0] * r]]
    h = n // 2
    rng = range(h)
    a = inv_sym([row[:h] for row in m[:h]])
    f = [row[h:] for row in m[:h]]
    af = [[total([a[i][l] * f[l][j] for l in rng]) for j in rng] for i in rng]
    s = inv_sym(sym(lambda i, j: m[h + i][h + j] - total([f[l][i] * af[l][j] for l in rng]), h))
    off = [[-total([af[i][l] * s[l][j] for l in rng]) for j in rng] for i in rng]
    top = sym(lambda i, j: a[i][j] - total([off[i][l] * af[j][l] for l in rng]), h)
    return [top[i] + off[i] for i in rng] + [[off[j][i] for j in rng] + s[i] for i in rng]


def sweep(p, b, late):
    n = p.shape[0]
    sub = lax.broadcasted_iota(jnp.int32, (n, n), 0)
    lane = lax.broadcasted_iota(jnp.int32, (n, n), 1)
    lane1 = lane[0:1]
    for k in range(0, n, b):
        if k == 3 * n // 4:
            late()
        c = [jnp.broadcast_to(p[:, k + j : k + j + 1], (n, n)) for j in range(b)]
        m = inv_sym(sym(lambda i, j: c[j][k + i : k + i + 1], b))
        r = [
            jnp.where(lane1 == k + j, -1.0, jnp.where(lane1 // b == k // b, 0.0, p[k + j : k + j + 1]))
            for j in range(b)
        ]
        w = [total([m[i][j] * r[j] for j in range(b)]) for i in range(b)]
        c = [jnp.where(sub == k + j, -1.0, jnp.where(sub // b == k // b, 0.0, c[j])) for j in range(b)]
        keep = jnp.where((sub // b == k // b) | (lane // b == k // b), 0.0, p)
        p = keep - total([c[j] * w[j] for j in range(b)])
    return p


def negative_inverse(a, nb, b, between):
    n = a.shape[0]
    sub = lax.broadcasted_iota(jnp.int32, (n, n), 0) // nb
    lane = lax.broadcasted_iota(jnp.int32, (n, n), 1) // nb
    square = (nb, nb)
    eye = (
        lax.broadcasted_iota(jnp.int32, square, 0) == lax.broadcasted_iota(jnp.int32, square, 1)
    ).astype(jnp.float32)
    for i in range(n // nb):
        s = i * nb
        rows = a[s : s + nb]
        neg = sweep(rows[:, s : s + nb], b, lambda: between(2 * i))
        if i == n // nb - 1:
            between(2 * i + 1)
        w = -hdot(neg, rows)

        def parts(middle, full):
            left = [full[:, :s]] if s else []
            right = [full[:, s + nb :]] if s + nb < n else []
            return jnp.concatenate(left + [middle] + right, axis=1)

        a = jnp.where((sub == i) | (lane == i), 0.0, a) - hdot(parts(-eye, rows), parts(neg, w), TN)
        between(2 * i + 1 + i // (n // nb - 1))
    return a


class Place:
    def __init__(self):
        me = lax.axis_index("vert")
        self.core = lax.rem(me, 2)
        self.y = lax.rem(me // 2, NY)
        self.x = me // (2 * NY)
        self.z = lax.axis_index("frame")
        self.xs = [lax.rem(self.x + k, NX) for k in range(NX)]
        self.ys = [lax.rem(self.y + k, NY) for k in range(NY)]
        self.zs = [lax.rem(self.z + k, NZ) for k in range(NZ)]
        vert = lambda x, y, core: {"vert": (x * NY + y) * 2 + core}
        self.sib = vert(self.x, self.y, 1 - self.core)
        self.xp = [vert(a, self.y, self.core) for a in self.xs]
        self.yp = [vert(self.x, a, self.core) for a in self.ys]
        self.zp = [{"frame": a} for a in self.zs]


def send(src, dst, s, r, peer):
    cp = pltpu.make_async_remote_copy(src, dst, s, r, device_id=peer, device_id_type=MESH)
    cp.start()
    return cp


def reduce_steps(pos, d, bufs, sems, sent):
    b0, acc, b1, sub, b2, gat, full = bufs
    whole_y = gat is None
    (s0, r0), (s1, r1), (s2, r2), (s3, r3), (s4, r4), (s5, r5) = sems
    half = d.shape[0] // 2
    q = half // NX
    e = b2.shape[1]
    xs, ys, core = pos.xs, pos.ys, pos.core
    order = (2, 1, 3, 0)
    c0 = [
        send(d.at[pl.ds((1 - core) * half + xs[k] * q, q)], b0.at[i], s0.at[i], r0.at[i], pos.sib)
        for i, k in enumerate(order)
    ]
    sent += c0
    yield
    c1 = {}
    for i, k in enumerate(order):
        c0[i].wait_recv()
        acc[i] = b0[i] + d[pl.ds(core * half + xs[k] * q, q)]
        if k:
            c1[k] = send(acc.at[i], b1.at[k - 1], s1.at[k - 1], r1.at[k - 1], pos.xp[k])
    sent += c1.values()
    yield
    tot = acc[3]
    for k in (1, 3, 2):
        c1[k].wait_recv()
        tot = tot + b1[k - 1]
    sub[0:q] = tot
    if not whole_y and NY * e > q:
        sub[q:] = jnp.zeros((NY * e - q, 8, 128), jnp.float32)
    if whole_y:
        b2[pos.y] = tot
    c2 = {
        k: send(
            sub if whole_y else sub.at[pl.ds(ys[k] * e, e)], b2.at[pos.y if whole_y else k - 1],
            s2.at[k - 1], r2.at[k - 1], pos.yp[k],
        )
        for k in far_first
    }
    sent += c2.values()
    yield
    for k in far_first[::-1]:
        c2[k].wait_recv()
    tot = b2[0]
    for k in range(1, b2.shape[0]):
        tot = tot + b2[k]
    if not whole_y:
        mine = pl.ds(pos.y * e, e)
        tot = tot + sub[mine]
        gat[mine] = tot
        c3 = {
            k: send(gat.at[mine], gat.at[mine], s3.at[k - 1], r3.at[k - 1], pos.yp[k])
            for k in far_first
        }
        sent += c3.values()
        yield
        for k in far_first[::-1]:
            c3[k].wait_recv()
        tot = gat[0:q]
    mine = pl.ds(core * half + pos.x * q, q)
    full[mine] = tot
    c4 = {k: send(full.at[mine], full.at[mine], s4.at[k - 1], r4.at[k - 1], pos.xp[k]) for k in (2, 1, 3)}
    c5 = [send(full.at[mine], full.at[mine], s5.at[0], r5.at[0], pos.sib)]
    sent += c4.values()
    yield
    for i, k in enumerate((1, 3, 2)):
        c4[k].wait_recv()
        blk = pl.ds(core * half + lax.rem(pos.x + NX - k, NX) * q, q)
        c5.append(send(full.at[blk], full.at[blk], s5.at[i + 1], r5.at[i + 1], pos.sib))
    sent += c5
    yield
    for cp in c5:
        cp.wait_recv()
    yield


def kernel(ridge, scale, *refs):
    it = iter(refs)
    take = lambda n: [next(it) for _ in range(n)]
    anim, rest_h, lab_h, prior_h, out, f_out = take(6)
    rows, feats, rest, lab, w_ref, dg, dr, g, gb = take(9)
    ez, ey, ex, ec, et = take(5)
    g_bufs, r_bufs = take(6), take(7)
    g_bufs.insert(5, None)
    in_sem, row_sem = take(2)
    pairs = lambda n: [tuple(take(2)) for _ in range(n)]
    g_sems, r_sems = pairs(6), pairs(6)
    (sg, rg), (sa, ra), (sz, rz), (sy, ry), (sx, rx), (sc, rc) = pairs(6)

    n_rows, verts = anim.shape
    bones = prior_h.shape[0]
    joint = 4 * bones
    cv = verts // CHUNKS
    pos = Place()

    barrier = pltpu.get_barrier_semaphore()
    peers = [pos.sib] + pos.xp[1:] + pos.yp[1:] + pos.zp[1:]
    for p in peers:
        pl.semaphore_signal(barrier, inc=1, device_id=p, device_id_type=MESH)
    small = [
        pltpu.make_async_copy(src, dst, in_sem.at[i])
        for i, (src, dst) in enumerate(((prior_h, w_ref), (rest_h, rest), (lab_h, lab)))
    ]
    for cp in small:
        cp.start()
    for j in range(CHUNKS):
        s = pl.ds(j * cv, cv)
        pltpu.make_async_copy(anim.at[:, s], rows.at[:, s], row_sem.at[j]).start()
    for cp in small:
        cp.wait()

    ids = lax.broadcasted_iota(jnp.int32, (bones, cv), 0)

    def gram_chunk(j, gram):
        s = pl.ds(pl.multiple_of(j * cv, cv), cv)
        summed = jnp.where(ids == lab[:, s], 1.0, 0.0) + w_ref[:, s]
        w = summed / jnp.sum(summed, axis=0, keepdims=True)
        w_ref[:, s] = w
        f = jnp.concatenate([w * rest[k : k + 1, s] for k in range(3)] + [w], axis=0)
        feats[:, s] = f
        return gram + hdot(f, f, NT)

    gram = lax.fori_loop(0, CHUNKS, gram_chunk, jnp.zeros((joint, joint), jnp.float32))
    rt = n_rows // 8
    bt = bones // 8
    last = jnp.concatenate([gram[bones : 2 * bones, bones : 2 * bones], gram[3 * bones :, 3 * bones :]], axis=1)
    packed = [gram[:bones, :128], gram[:bones, 128:], gram[bones : 2 * bones, 128:], gram[2 * bones : 3 * bones, 128:], last]
    for i, part in enumerate(packed):
        dg[i * bt : (i + 1) * bt] = part.reshape(bt, 8, 128)
    sent = []
    pl.semaphore_wait(barrier, len(peers))
    gsteps = reduce_steps(pos, dg, g_bufs, g_sems, sent)
    rsteps = reduce_steps(pos, dr, r_bufs, r_sems, sent)
    next(gsteps)

    def rhs_chunk(j, rhs):
        s = pl.ds(pl.multiple_of(j * cv, cv), cv)
        pltpu.make_async_copy(anim.at[:, s], rows.at[:, s], row_sem.at[j]).wait()
        return rhs + hdot(rows[:, s], feats[:, s], NT)

    rhs = lax.fori_loop(0, 1, rhs_chunk, jnp.zeros((n_rows, joint), jnp.float32))
    next(gsteps)
    rhs = lax.fori_loop(1, CHUNKS, rhs_chunk, rhs)
    for h in range(2):
        dr[h * rt : (h + 1) * rt] = rhs[:, h * 128 : (h + 1) * 128].reshape(rt, 8, 128)
    next(rsteps)
    next(rsteps)
    next(gsteps)
    next(rsteps)
    next(gsteps)
    next(rsteps)
    next(gsteps)
    next(gsteps)

    square = (joint, joint)
    eye = lax.broadcasted_iota(jnp.int32, square, 0) == lax.broadcasted_iota(jnp.int32, square, 1)
    dg, dr = g_bufs[-1], r_bufs[-1]
    p = [dg[i * bt : (i + 1) * bt].reshape(bones, 128) for i in range(5)]
    blocks = {}
    pairs_of = (((0, 0), (0, 1)), ((0, 2), (0, 3)), ((1, 2), (1, 3)), ((2, 2), (2, 3)), ((1, 1), (3, 3)))
    for part, names in zip(p, pairs_of):
        for i, (k, l) in enumerate(names):
            blocks[k, l] = blocks[l, k] = part[:, i * bones : (i + 1) * bones]
    gram = jnp.concatenate(
        [jnp.concatenate([blocks[k, l] for l in range(4)], axis=1) for k in range(4)], axis=0
    )
    gram = gram + jnp.where(eye, ridge, 0.0)
    neg = negative_inverse(gram, 64, 4, lambda i: next(rsteps) if i in (2, 7, 8) else None)
    rhs = jnp.concatenate([dr[h * rt : (h + 1) * rt].reshape(n_rows, 128) for h in range(2)], axis=1)
    neg_parts = halves(neg)
    tt = -dot3(halves(rhs), neg_parts)
    tt = tt - dot3(halves(rhs - hdot(tt, gram)), neg_parts)
    t_parts = halves(tt.T)

    def fit_chunk(j, squares):
        s = pl.ds(pl.multiple_of(j * cv, cv), cv)
        e = rows[:, s] - hdot(tt, feats[:, s])
        pulled = dot3(t_parts, halves(e))
        grad = pulled[3 * bones :]
        for k in range(3):
            grad = grad + pulled[k * bones : (k + 1) * bones] * rest[k : k + 1, s]
        g[:, :, s] = (-2.0 * grad).reshape(NZ, bones // NZ, cv)
        for k in far_first:
            send(g.at[pos.zs[k], :, s], gb.at[k - 1, :, s], sg.at[j, k - 1], rg.at[j, k - 1], pos.zp[k])
        sq = (e * e).reshape(n_rows // 8, 8, cv).sum(axis=0)
        return squares + total([sq[:, i * 128 : (i + 1) * 128] for i in range(cv // 128)])

    et[0] = lax.fori_loop(0, CHUNKS, fit_chunk, jnp.zeros((8, 128), jnp.float32))
    cz = [send(et.at[0], ez.at[pos.z], sz.at[k - 1], rz.at[k - 1], pos.zp[k]) for k in far_first]

    mine = pl.ds(pl.multiple_of(pos.z * (bones // NZ), bones // NZ), bones // NZ)

    def update_chunk(j, carry):
        s = pl.ds(pl.multiple_of(j * cv, cv), cv)
        grad = g[pos.z, :, s]
        for k in far_first[::-1]:
            pltpu.make_async_remote_copy(
                g.at[pos.zs[k], :, s], gb.at[k - 1, :, s], sg.at[j, k - 1], rg.at[j, k - 1],
                device_id=pos.zp[k], device_id_type=MESH,
            ).wait()
            grad = grad + gb[k - 1, :, s]
        out[pos.z, :, s] = jnp.clip(w_ref[mine, s] - step_size * grad, 0.0, 1.0)
        for k in far_first:
            send(out.at[pos.z, :, s], out.at[pos.z, :, s], sa.at[j, k - 1], ra.at[j, k - 1], pos.zp[k])
        return carry

    lax.fori_loop(0, CHUNKS, update_chunk, 0)

    def add_up(copies, buf, at, i):
        buf[at] = et[i]
        for cp in copies:
            cp.wait_recv()
        tot = buf[0]
        for k in range(1, buf.shape[0]):
            tot = tot + buf[k]
        et[i + 1] = tot

    add_up(cz, ez, pos.z, 0)
    cy = [send(et.at[1], ey.at[pos.y], sy.at[k - 1], ry.at[k - 1], pos.yp[k]) for k in far_first]
    add_up(cy, ey, pos.y, 1)
    cx = [send(et.at[2], ex.at[pos.x], sx.at[k - 1], rx.at[k - 1], pos.xp[k]) for k in (2, 1, 3)]
    add_up(cx, ex, pos.x, 2)
    cc = [send(et.at[3], ec.at[0], sc.at[0], rc.at[0], pos.sib)]
    cc[0].wait_recv()
    et[4] = et[3] + ec[0]
    f_out[...] = jnp.sum(et[4], axis=(0, 1), keepdims=True) * scale

    def gather_chunk(j, carry):
        s = pl.ds(pl.multiple_of(j * cv, cv), cv)
        for k in far_first[::-1]:
            pltpu.make_async_remote_copy(
                out.at[pos.z, :, s], out.at[pos.z, :, s], sa.at[j, k - 1], ra.at[j, k - 1],
                device_id=pos.zp[k], device_id_type=MESH,
            ).wait()
        return carry

    for cp in sent + cz + cy + cx + cc:
        cp.wait_send()
    lax.fori_loop(0, CHUNKS, gather_chunk, 0)


def local(animated, rest_positions, labels, weight_prior):
    bones, verts = weight_prior.shape
    n_rows = 3 * animated.shape[0]
    joint = 4 * bones
    verts_total = verts * lax.axis_size("vert")
    frames_total = animated.shape[0] * lax.axis_size("frame")
    rows = animated.transpose(1, 0, 2).reshape(n_rows, verts)

    vmem = lambda *s: pltpu.VMEM(s, jnp.float32)
    tiles = lambda *s: vmem(*s, 8, 128)

    def buffers(n, whole_y):
        q = n // (2 * NX)
        e = -(-q // NY)
        common = [tiles(NX, q), tiles(NX, q), tiles(NX - 1, q)]
        if whole_y:
            return common + [tiles(q), tiles(NY, q), tiles(n)]
        return common + [tiles(NY * e), tiles(NY - 1, e), tiles(NY * e), tiles(n)]

    pair = lambda *s: [pltpu.SemaphoreType.DMA(s)] * 2
    reduce_pairs = pair(4) + pair(3) + pair(7) + pair(7) + pair(3) + pair(4)
    n_gram, n_rhs = 10 * bones * bones // 1024, n_rows * joint // 1024
    scratch = [
        vmem(n_rows, verts), vmem(joint, verts),
        vmem(3, verts), pltpu.VMEM((1, verts), jnp.int32),
        vmem(bones, verts), tiles(n_gram), tiles(n_rhs), vmem(NZ, bones // NZ, verts),
        vmem(NZ - 1, bones // NZ, verts), tiles(NZ), tiles(NY), tiles(NX), tiles(1), tiles(5),
    ]
    scratch += buffers(n_gram, True) + buffers(n_rhs, False)
    scratch += [pltpu.SemaphoreType.DMA((3,)), pltpu.SemaphoreType.DMA((CHUNKS,))]
    scratch += reduce_pairs + reduce_pairs
    scratch += pair(CHUNKS, NZ - 1) + pair(CHUNKS, NZ - 1) + pair(NZ - 1) + pair(NY - 1) + pair(NX - 1) + pair(1)

    hbm, vm = pl.BlockSpec(memory_space=pltpu.HBM), pl.BlockSpec(memory_space=pltpu.VMEM)
    new_weights, fit_error = pl.pallas_call(
        functools.partial(kernel, ridge_scale * verts_total, 1.0 / (3.0 * frames_total * verts_total)),
        out_shape=(
            jax.ShapeDtypeStruct((NZ, bones // NZ, verts), jnp.float32),
            jax.ShapeDtypeStruct((1, 1), jnp.float32),
        ),
        in_specs=[hbm] * 4,
        out_specs=(vm, vm),
        scratch_shapes=scratch,
        compiler_params=pltpu.CompilerParams(
            collective_id=0, has_side_effects=True, vmem_limit_bytes=28 << 20
        ),
        name="skinning",
    )(*[pltpu.with_memory_space_constraint(a, pltpu.HBM) for a in (rows, rest_positions, labels.reshape(1, verts), weight_prior)])
    return new_weights.reshape(bones, verts), fit_error.reshape(())


def solution(mesh):
    placed = (P("frame", None, "vert"), P(None, "vert"), P("vert"), P(None, "vert"))
    return jax.shard_map(
        local, mesh=mesh, in_specs=placed, out_specs=(P(None, "vert"), P()), check_vma=False
    )
```
